32 devices in a mesh: groups: 2 (over y), rows: 4 (over z), cols: 2 (over x), sub: 2 (over core).
Axes of the slice: x: 2, y: 2, z: 4, core: 2. Of those that a mesh axis runs over, the one named last changes fastest.
Arguments:
- diagonal_tiles: float32 [256, 128, 128], P(('groups', 'rows', 'sub')), parts along dimension 0
- coupling_tiles: float32 [256, 6, 128, 128], P(('groups', 'rows', 'sub'), 'cols'), parts along dimension 0, may hold values from -0.0625 to 0.0625
- column_part: int32 [256, 6], P(('groups', 'rows', 'sub'), 'cols'), parts along dimension 0, may hold values from 0 to 4
- column_tile: int32 [256, 6], P(('groups', 'rows', 'sub'), 'cols'), parts along dimension 0, may hold values from 0 to 31
- neighbours: int32 [8, 4], P('groups'), parts along dimension 0, may hold values from 0 to 3, as said below
- right_side: float32 [256, 128], P(('groups', 'rows', 'sub')), parts along dimension 0, may hold values from -6 to 6
- jacobi_inverse: float32 [256, 128, 128], P(('groups', 'rows', 'sub')), parts along dimension 0, as said below
Outputs:
- solution: float32 [256, 128], P(('groups', 'rows', 'sub')), parts along dimension 0
- residual: float32 [256, 128], P(('groups', 'rows', 'sub')), parts along dimension 0
The draws below stay inside these ranges and needn't reach their ends.
There are 2 independent parts, one for each index of `groups`. The reference program is written for one: setup_inputs(seed, part) draws one part's arguments, and reference() takes and returns one part's arrays. A program takes and returns all parts, laid end to end along the dimension named above; each array names one. Nothing has to cross between parts.
Inputs may be any that keep to these rules, and one draw needn't show every extreme that they name: `neighbours`: entry 0 of partition p's list is (p + 4 // 2) mod 4, the opposite partition on the cycle; every other entry names a partition whose index differs from p by 1 to 2 (without wrapping round); entries may repeat. `jacobi_inverse`: block-diagonal: each group of 5 consecutive variables, from the first on, forms one 5 x 5 block, and each variable left over after the last whole group of 5 is a 1 x 1 block of its own.
All inputs are finite; a program needn't handle non-finite values.
Results may differ from the reference program's by a relative error of at most 0.00019.
Values sent between devices are 32-bit elements; how exact they have to be, the bound alone decides.
No kernel may reach another device: no remote copies, remote signals or barrier semaphores. Data moves between devices by JAX's collectives and lax.ppermute only.
A program may use at most 64 MiB of HBM per device.

```python
import jax
import jax.numpy as jnp
from jax import lax

TW = 128
NR = 2
ITERS = 2
RB = 32
NB = 128
K = 6
NNB = 4
N_ROWS = 4


def draw_diagonal_tiles(key, part):
    first, second = jax.random.split(jax.random.fold_in(key, 11))
    scales = jax.random.uniform(first, (NB, TW, 1), jnp.float32, 1.5, 2.5)
    noise = jax.random.normal(second, (NB, TW, TW), jnp.float32)
    return scales * jnp.eye(TW, dtype=jnp.float32) + 0.3 / TW ** 0.5 * noise


def draw_jacobi_inverse(key, part):
    first, second = jax.random.split(jax.random.fold_in(key, 23))
    index = jnp.arange(TW, dtype=jnp.int32)
    cutoff = TW // 5 * 5
    blocks = jnp.where(index < cutoff, index // 5, TW + index)
    inside = (blocks[:, None] == blocks[None, :]).astype(jnp.float32)
    scales = jax.random.uniform(first, (NB, TW, 1), jnp.float32, 0.4, 1.0)
    noise = jax.random.normal(second, (NB, TW, TW), jnp.float32) * 0.15
    return (scales * jnp.eye(TW, dtype=jnp.float32) + noise) * inside


def draw_neighbours(key, part):
    picked = jax.random.randint(jax.random.fold_in(key, 37), (N_ROWS, NNB), 0, NNB)
    offset = jnp.where(picked < NR, picked - NR, picked - NR + 1)
    owner = jnp.arange(N_ROWS, dtype=jnp.int32)[:, None]
    target = owner + offset
    target = jnp.where((target < 0) | (target >= N_ROWS), owner - offset, target)
    opposite = (owner + N_ROWS // 2) % N_ROWS
    column = jnp.arange(NNB, dtype=jnp.int32)[None, :]
    target = jnp.where(column == 0, opposite, target)
    return target.astype(jnp.int32)


def set_ends(entries, key, smallest, largest):
    dims = entries.shape
    index_at = [jax.random.randint(jax.random.fold_in(key, axis), (), 0, dims[axis]) for axis in range(len(dims))]
    entries = entries.at[tuple(index_at)].set(smallest)
    longest = dims.index(max(dims))
    index_at[longest] = (index_at[longest] + 1) % dims[longest]
    return entries.at[tuple(index_at)].set(largest)


def level_of(key, dims, shards, least, largest):
    level = 1.0
    for axis_at, parts in shards:
        steps = jax.random.uniform(jax.random.fold_in(jax.random.fold_in(key, 6), axis_at), (parts,), jnp.float32, least / len(shards), largest / len(shards))
        level = level * jnp.repeat(jnp.exp(steps), dims[axis_at] // parts).reshape((-1,) + (1,) * (len(dims) - 1 - axis_at))
    return level


def gaussian(own_key, extent, deviation, limit, cuts=(), kind=jnp.bfloat16):
    result = deviation * jax.random.normal(own_key, extent, jnp.float32)
    if cuts:
        result = result * level_of(own_key, extent, cuts, -0.22, 0.18)
    return jnp.clip(result, -limit, limit).astype(kind)


def setup_inputs(seed: int = 0, part: int = 0) -> dict:
    splits = jax.random.split(jax.random.key(seed), 8)
    part_splits = jax.random.split(jax.random.fold_in(splits[7], part), 8)
    diagonal_tiles = draw_diagonal_tiles(jax.random.fold_in(jax.random.fold_in(splits[7], part), 71), part)
    coupling_tiles = gaussian(part_splits[1], (NB, K, TW, TW), (11 * K * TW) ** -0.5, 0.0625, ((0, 8), (1, 2)), jnp.float32)
    column_part = set_ends(jax.random.randint(part_splits[2], (NB, K), 0, NNB + 1), jax.random.fold_in(part_splits[2], 1), 0, NNB).astype(jnp.int32)
    column_tile = set_ends(jax.random.randint(part_splits[3], (NB, K), 0, RB), jax.random.fold_in(part_splits[3], 1), 0, RB - 1).astype(jnp.int32)
    neighbours = draw_neighbours(jax.random.fold_in(jax.random.fold_in(splits[7], part), 71), part)
    right_side = gaussian(part_splits[5], (NB, TW), 1.0, 6.0, ((0, 8),), jnp.float32)
    jacobi_inverse = draw_jacobi_inverse(jax.random.fold_in(jax.random.fold_in(splits[7], part), 71), part)
    return dict(diagonal_tiles=diagonal_tiles, coupling_tiles=coupling_tiles, column_part=column_part, column_tile=column_tile, neighbours=neighbours, right_side=right_side, jacobi_inverse=jacobi_inverse)


def transpose_apply(vector, diagonal_tiles, coupling_tiles, column_part, column_tile, neighbours):
    highest = lax.Precision.HIGHEST
    diagonal_part = jnp.einsum('rij,ri->rj', diagonal_tiles, vector, precision=highest)
    partial_value = jnp.einsum('rkij,ri->rkj', coupling_tiles, vector, precision=highest)
    tile_rows = vector.shape[0]
    part_rows = tile_rows // N_ROWS
    owner = jnp.arange(tile_rows, dtype=jnp.int32) // part_rows
    listed = neighbours[owner]
    chosen = jnp.take_along_axis(listed, jnp.maximum(column_part - 1, 0).astype(jnp.int32), axis=1)
    target = jnp.where(column_part == 0, owner[:, None], chosen)
    landing = (target * part_rows + column_tile).astype(jnp.int32).reshape(-1)
    summed = jax.ops.segment_sum(partial_value.reshape(-1, partial_value.shape[-1]), landing, num_segments=tile_rows)
    return diagonal_part + summed


def precondition(jacobi_inverse, vector):
    return jnp.einsum('rij,ri->rj', jacobi_inverse, vector, precision=lax.Precision.HIGHEST)


def reference(diagonal_tiles, coupling_tiles, column_part, column_tile, neighbours, right_side, jacobi_inverse):
    def apply_a(vector):
        return transpose_apply(vector, diagonal_tiles, coupling_tiles, column_part, column_tile, neighbours)

    solution = jnp.zeros_like(right_side)
    residual = right_side
    shadow = right_side
    search = right_side
    rho_now = jnp.sum(shadow * residual)
    for step in range(ITERS):
        search_hat = precondition(jacobi_inverse, search)
        image = apply_a(search_hat)
        alpha = rho_now / jnp.sum(shadow * image)
        half = residual - alpha * image
        half_hat = precondition(jacobi_inverse, half)
        twice = apply_a(half_hat)
        omega = jnp.sum(twice * half) / jnp.sum(twice * twice)
        solution = solution + alpha * search_hat + omega * half_hat
        residual = half - omega * twice
        if step + 1 < ITERS:
            rho_next = jnp.sum(shadow * residual)
            search = residual + (rho_next / rho_now) * (alpha / omega) * (search - omega * image)
            rho_now = rho_next
    return solution, residual
```

```python
import functools

import jax
import jax.numpy as jnp
from jax import lax
from jax.experimental import pallas as pl
from jax.experimental.pallas import tpu as pltpu
from jax.sharding import PartitionSpec as P

BLOCK = 5
BAND = BLOCK - 1
LANES = 128
PART = ("rows", "cols", "sub")


def apply_m(band_ref, v):
    width = v.shape[1]
    z = band_ref[BAND] * v
    for d in range(-BAND, BAND + 1):
        if d:
            z = z + band_ref[d + BAND] * pltpu.roll(v, (-d) % width, 1)
    return z


def split3(x):
    hi = x.astype(jnp.bfloat16)
    rest = x - hi.astype(jnp.float32)
    mid = rest.astype(jnp.bfloat16)
    low = (rest - mid.astype(jnp.float32)).astype(jnp.bfloat16)
    return jnp.concatenate([hi, mid, low], axis=0)


def products(z, coupling_ref, diagonal_ref, partial_ref, own_ref):
    rows, slots = coupling_ref.shape[0], coupling_ref.shape[1]
    z_t = z.T
    for r in range(rows):
        column = jnp.broadcast_to(z_t[:, r : r + 1], coupling_ref.shape[2:])
        for k in range(slots):
            partial_ref[pl.ds(k * rows + r, 1), :] = jnp.sum(column * coupling_ref[r, k], axis=0, keepdims=True)
        own_ref[pl.ds(r, 1), :] = jnp.sum(column * diagonal_ref[r], axis=0, keepdims=True)


def emit(z, tail, spread_ref, coupling_ref, diagonal_ref, partial_ref, own_ref, send_ref):
    rows = z.shape[0]
    products(z, coupling_ref, diagonal_ref, partial_ref, own_ref)
    send_ref[...] = jnp.dot(spread_ref[...], split3(partial_ref[...]), preferred_element_type=jnp.float32)
    for d in range(send_ref.shape[0] // (rows + 1)):
        send_ref[pl.ds(d * (rows + 1) + rows, 1), :] = tail


def pack(scalars, width):
    lane = lax.broadcasted_iota(jnp.int32, (1, width), 1)
    tail = jnp.zeros((1, width), jnp.float32)
    for at, value in enumerate(scalars):
        tail = jnp.where(lane == at, value, tail)
    return tail


def total(x):
    return jnp.sum(jnp.sum(x, axis=0, keepdims=True), axis=1, keepdims=True)


def peak(x):
    return jnp.max(jnp.max(jnp.abs(x), axis=0, keepdims=True), axis=1, keepdims=True)


def level(x, like):
    size, aim = peak(x), peak(like)
    good = (size > 0) & (aim > 0)
    return jnp.where(good, aim / size, 1.0), jnp.where(good, size / aim, 1.0)


def gather_tails(recv_ref, rows):
    count = recv_ref.shape[0] // (rows + 1)
    return [recv_ref[pl.ds(d * (rows + 1) + rows, 1), :] for d in range(count)]


def chunk(recv_ref, d, rows):
    return recv_ref[pl.ds(d * (rows + 1), rows), :]


def first_kernel(
    b_ref, jacobi_ref, part_ref, tile_ref, near_ref, coupling_ref, diagonal_ref,
    send_ref, own_ref, band_ref, spread_ref, partial_ref, *, sizes,
):
    n_rows, n_cols, n_sub = sizes
    rows, slots = coupling_ref.shape[0], coupling_ref.shape[1]
    width = b_ref.shape[1]
    folded = jnp.sum(jacobi_ref[...].reshape(rows, width // 8, 8, width), axis=1)
    m = lax.broadcasted_iota(jnp.int32, (1, 8, width), 1)
    j = lax.broadcasted_iota(jnp.int32, (1, 8, width), 2)
    last = width // BLOCK * BLOCK
    for d in range(-BAND, BAND + 1):
        i = j + d
        inside = (i // BLOCK == j // BLOCK) & (j < last) if d else j >= 0
        picked = inside & (i >= 0) & (lax.rem(i + 8, 8) == m)
        band_ref[d + BAND] = jnp.sum(jnp.where(picked, folded, 0.0), axis=1)
    own = lax.axis_index("rows")
    part, tile = part_ref[...], tile_ref[...]
    near = near_ref[...]
    near_row = lax.broadcasted_iota(jnp.int32, near.shape, 0)
    mine = jnp.sum(jnp.where(near_row == own, near, 0), axis=0, keepdims=True)
    target = jnp.where(part == 0, own, 0)
    for n in range(near.shape[1]):
        target = target + jnp.where(part == n + 1, mine[:, n : n + 1], 0)
    landing = target * (rows * n_sub) + tile
    lanes = -(-spread_ref.shape[0] // LANES) * LANES
    at = lax.broadcasted_iota(jnp.int32, (rows, lanes), 1)
    device, line = at // (rows + 1), at % (rows + 1)
    row, sub = device // (n_cols * n_sub), device % n_sub
    wanted = jnp.where((line < rows) & (row < n_rows), row * (rows * n_sub) + sub * rows + line, -1)
    hits = jnp.concatenate(
        [(landing[:, k : k + 1] == wanted).astype(jnp.float32) for k in range(slots)], axis=0
    )
    one_hot = hits.T[: spread_ref.shape[0]].astype(jnp.bfloat16)
    spread_ref[...] = jnp.concatenate([one_hot] * 3, axis=1)
    z = apply_m(band_ref, b_ref[...])
    emit(z, jnp.zeros((1, width), jnp.float32), spread_ref, coupling_ref, diagonal_ref, partial_ref, own_ref, send_ref)


def second_kernel(
    recv_ref, own_in, b_ref, band_ref, spread_ref, coupling_ref, diagonal_ref,
    send_ref, own_ref, q_ref, partial_ref,
):
    b = b_ref[...]
    rows, width = b.shape
    q = own_in[...]
    for d in range(recv_ref.shape[0] // (rows + 1)):
        q = q + chunk(recv_ref, d, rows)
    q_ref[...] = q
    up, down = level(q, b)
    tail = pack([total(b * b), total(b * q), down], width)
    z = apply_m(band_ref, q * up)
    emit(z, tail, spread_ref, coupling_ref, diagonal_ref, partial_ref, own_ref, send_ref)


def scalars_of(recv_ref, rows, count, repeats):
    tails = gather_tails(recv_ref, rows)
    summed = functools.reduce(jnp.add, tails)
    return tails, [summed[:, n : n + 1] / repeats for n in range(count)]


def weighted(recv_ref, own_in, own_down, tails, at, factor):
    rows = own_in.shape[0]
    out = own_in[...] * (factor * own_down)
    for d, tail in enumerate(tails):
        out = out + chunk(recv_ref, d, rows) * (factor * tail[:, at : at + 1])
    return out


def third_kernel(
    recv_ref, own_in, b_ref, q_ref, band_ref, spread_ref, coupling_ref, diagonal_ref,
    send_ref, own_ref, twice_ref, half_ref, u_ref, keep_ref, partial_ref, *, n_cols,
):
    b, q = b_ref[...], q_ref[...]
    rows, width = b.shape
    tails, (rho, cross) = scalars_of(recv_ref, rows, 2, n_cols)
    alpha = rho / cross
    _, down = level(q, b)
    u = weighted(recv_ref, own_in, down, tails, 2, alpha)
    twice = q - u
    half = b - alpha * q
    up, down = level(twice, half)
    tail = pack([total(twice * half), total(twice * twice), total(b * half), total(b * twice), down], width)
    twice_ref[...], half_ref[...], u_ref[...] = twice, half, u
    keep_ref[...] = pack([rho, alpha], width)
    z = apply_m(band_ref, twice * up)
    emit(z, tail, spread_ref, coupling_ref, diagonal_ref, partial_ref, own_ref, send_ref)


def fourth_kernel(
    recv_ref, own_in, b_ref, q_ref, twice_ref, half_ref, u_ref, keep_ref, band_ref, spread_ref, coupling_ref,
    diagonal_ref, send_ref, own_ref, a_ref, residual_ref, image_ref, search_ref, done_ref, kept_ref, partial_ref,
    *, n_cols,
):
    b, q, twice, half = b_ref[...], q_ref[...], twice_ref[...], half_ref[...]
    rows, width = b.shape
    rho, alpha = keep_ref[:, 0:1], keep_ref[:, 1:2]
    tails, (cross, square, b_half, b_twice) = scalars_of(recv_ref, rows, 4, n_cols)
    omega = cross / square
    rho_next = b_half - omega * b_twice
    ratio = rho_next / rho
    beta = ratio * (alpha / omega)
    _, down = level(twice, half)
    a = twice - weighted(recv_ref, own_in, down, tails, 4, omega)
    residual = half - omega * twice
    image = a + beta * q - ratio * u_ref[...]
    up, down = level(image, residual)
    tail = pack([total(b * image), down], width)
    a_ref[...], residual_ref[...], image_ref[...] = a, residual, image
    search_ref[...] = residual + beta * (b - omega * q)
    done_ref[...] = alpha * b + omega * half
    kept_ref[...] = pack([rho_next], width)
    z = apply_m(band_ref, image * up)
    emit(z, tail, spread_ref, coupling_ref, diagonal_ref, partial_ref, own_ref, send_ref)


def fifth_kernel(
    recv_ref, own_in, a_ref, residual_ref, image_ref, search_ref, done_ref, kept_ref,
    twice_ref, half_ref, sum_ref, dots_ref, *, n_cols,
):
    residual, image = residual_ref[...], image_ref[...]
    rows, width = residual.shape
    tails, (cross,) = scalars_of(recv_ref, rows, 1, n_cols)
    alpha = kept_ref[:, 0:1] / cross
    _, down = level(image, residual)
    twice = a_ref[...] - weighted(recv_ref, own_in, down, tails, 1, alpha)
    half = residual - alpha * image
    twice_ref[...], half_ref[...] = twice, half
    sum_ref[...] = done_ref[...] + alpha * search_ref[...]
    dots_ref[...] = pack([total(twice * half), total(twice * twice)], width)


def last_kernel(dots_ref, twice_ref, half_ref, sum_ref, band_ref, solution_ref, residual_ref):
    dots = dots_ref[...]
    omega = dots[:, 0:1] / dots[:, 1:2]
    half = half_ref[...]
    residual_ref[...] = half - omega * twice_ref[...]
    solution_ref[...] = apply_m(band_ref, sum_ref[...] + omega * half)


def partners(count, step):
    if count & (count - 1) == 0:
        return [(i, i ^ step) for i in range(count)]
    return [(i, (i + step) % count) for i in range(count)]


def sum_over(x, axis):
    count = lax.axis_size(axis)
    out = x
    for step in range(1, count):
        out = out + lax.ppermute(x, axis, partners(count, step))
    return out


def call(kernel, outs, args, scratch=()):
    spec = pl.BlockSpec(memory_space=pltpu.VMEM)
    return pl.pallas_call(
        kernel,
        out_shape=[jax.ShapeDtypeStruct(shape, kind) for shape, kind in outs],
        in_specs=[spec] * len(args),
        out_specs=[spec] * len(outs),
        scratch_shapes=list(scratch),
        compiler_params=pltpu.CompilerParams(vmem_limit_bytes=48 << 20),
    )(*args)


def on_device(diagonal, coupling, column_part, column_tile, neighbours, b, jacobi):
    f32 = jnp.float32
    rows, width = b.shape
    slots = coupling.shape[1]
    sizes = tuple(lax.axis_size(axis) for axis in PART)
    n_cols = sizes[1]
    devices = sizes[0] * sizes[1] * sizes[2]
    vec, line = ((rows, width), f32), ((1, width), f32)
    message = ((devices * (rows + 1), width), f32)
    band_shape = ((2 * BAND + 1, rows, width), f32)
    spread_shape = ((devices * (rows + 1), 3 * slots * rows), jnp.bfloat16)
    scratch = [pltpu.VMEM((slots * rows, width), f32)]

    def exchange(send):
        send = send.reshape(devices, rows + 1, 1, width)
        return lax.all_to_all(send, PART, 0, 0, tiled=True).reshape(devices * (rows + 1), width)

    send, own, band, spread = call(
        functools.partial(first_kernel, sizes=sizes), [message, vec, band_shape, spread_shape],
        (b, jacobi, column_part, column_tile, neighbours, coupling, diagonal), scratch,
    )
    fixed = (band, spread, coupling, diagonal)
    send, own, q = call(second_kernel, [message, vec, vec], (exchange(send), own, b) + fixed, scratch)
    send, own, twice, half, u, keep = call(
        functools.partial(third_kernel, n_cols=n_cols), [message] + [vec] * 4 + [line],
        (exchange(send), own, b, q) + fixed, scratch,
    )
    send, own, a, residual, image, search, done, kept = call(
        functools.partial(fourth_kernel, n_cols=n_cols), [message] + [vec] * 6 + [line],
        (exchange(send), own, b, q, twice, half, u, keep) + fixed, scratch,
    )
    twice, half, summed, dots = call(
        functools.partial(fifth_kernel, n_cols=n_cols), [vec] * 3 + [line],
        (exchange(send), own, a, residual, image, search, done, kept),
    )
    dots = sum_over(sum_over(dots, "sub"), "rows")
    return tuple(call(last_kernel, [vec, vec], (dots, twice, half, summed, band)))


def solution(mesh):
    lines = P(("groups", "rows", "sub"), None)
    tiles = P(("groups", "rows", "sub"), None, None)
    slots = P(("groups", "rows", "sub"), "cols")
    in_specs = (
        tiles, P(("groups", "rows", "sub"), "cols", None, None), slots, slots, P("groups", None), lines, tiles,
    )
    return jax.shard_map(on_device, mesh=mesh, in_specs=in_specs, out_specs=(lines, lines), check_vma=False)
```

```python
import functools

import jax
import jax.numpy as jnp
from jax import lax
from jax.experimental import pallas as pl
from jax.experimental.pallas import tpu as pltpu
from jax.sharding import PartitionSpec as P

BLOCK = 5
BAND = BLOCK - 1
LANES = 128
PART = ("rows", "cols", "sub")


def apply_m(band_ref, v):
    width = v.shape[1]
    z = band_ref[BAND] * v
    for d in range(-BAND, BAND + 1):
        if d:
            z = z + band_ref[d + BAND] * pltpu.roll(v, (-d) % width, 1)
    return z


def split3(x):
    hi = x.astype(jnp.bfloat16)
    rest = x - hi.astype(jnp.float32)
    mid = rest.astype(jnp.bfloat16)
    low = (rest - mid.astype(jnp.float32)).astype(jnp.bfloat16)
    return jnp.concatenate([hi, mid, low], axis=0)


def sum_lines(parts):
    line = lax.broadcasted_iota(jnp.int32, parts[0].shape, 0)
    step = 1
    while len(parts) > 1:
        low = (line // step) % 2 == 0
        parts = [
            jnp.where(low, one, two) + pltpu.roll(jnp.where(low, two, one), step, 0)
            for one, two in zip(parts[::2], parts[1::2])
        ]
        step *= 2
    return parts[0]


def products(z, coupling_ref, diagonal_ref, partial_ref, own_ref, column_ref, before=None):
    rows, slots, width = coupling_ref.shape[:3]
    for g in range(rows // 8):
        if before is not None:
            before(g)
        first = g * 8
        sums = [[] for _ in range(slots + 1)]
        for r in range(first, first + 8):
            column = jnp.broadcast_to(z[r : r + 1], (width, width)).T
            for k in range(slots):
                sums[k].append(jnp.sum((column * coupling_ref[r, k]).reshape(width // 8, 8, width), axis=0))
            sums[slots].append(jnp.sum((column * diagonal_ref[r]).reshape(width // 8, 8, width), axis=0))
        for k in range(slots):
            partial_ref[pl.ds(k * rows + first, 8), :] = sum_lines(sums[k])
        own_ref[pl.ds(first, 8), :] = sum_lines(sums[slots])


def emit(z, tail, spread_ref, coupling_ref, diagonal_ref, scratch, own_ref, send_ref, before=None):
    rows = z.shape[0]
    partial_ref, column_ref = scratch
    products(z, coupling_ref, diagonal_ref, partial_ref, own_ref, column_ref, before)
    send_ref[...] = jnp.dot(spread_ref[...], split3(partial_ref[...]), preferred_element_type=jnp.float32)
    for d in range(send_ref.shape[0] // (rows + 1)):
        send_ref[pl.ds(d * (rows + 1) + rows, 1), :] = tail


def pack(scalars, width):
    lane = lax.broadcasted_iota(jnp.int32, (1, width), 1)
    tail = jnp.zeros((1, width), jnp.float32)
    for at, value in enumerate(scalars):
        tail = jnp.where(lane == at, value, tail)
    return tail


def total(x):
    return jnp.sum(jnp.sum(x, axis=0, keepdims=True), axis=1, keepdims=True)


def peak(x):
    return jnp.max(jnp.max(jnp.abs(x), axis=0, keepdims=True), axis=1, keepdims=True)


def level(x, like):
    size, aim = peak(x), peak(like)
    good = (size > 0) & (aim > 0)
    return jnp.where(good, aim / size, 1.0), jnp.where(good, size / aim, 1.0)


def gather_tails(recv_ref, rows):
    count = recv_ref.shape[0] // (rows + 1)
    return [recv_ref[pl.ds(d * (rows + 1) + rows, 1), :] for d in range(count)]


def chunk(recv_ref, d, rows):
    return recv_ref[pl.ds(d * (rows + 1), rows), :]


def first_kernel(
    b_hbm, jacobi_hbm, part_hbm, tile_hbm, near_hbm, coupling_hbm, diagonal_hbm,
    send_ref, own_ref, band_ref, spread_ref, b_ref, coupling_ref, diagonal_ref,
    partial_ref, column_ref, jacobi_ref, part_ref, tile_ref, near_ref, small_sem, jacobi_sem, coupling_sem, diagonal_sem,
    *, sizes,
):
    n_rows, n_cols, n_sub = sizes
    rows, slots = coupling_ref.shape[0], coupling_ref.shape[1]
    width = b_ref.shape[1]
    groups = rows // 8

    def some(ref, g):
        return ref.at[pl.ds(g * 8, 8)]

    def copy_of(g, source, target, sem):
        return pltpu.make_async_copy(some(source, g), some(target, g), sem.at[g])

    small = [
        pltpu.make_async_copy(source, target, small_sem.at[n])
        for n, (source, target) in enumerate(
            ((b_hbm, b_ref), (part_hbm, part_ref), (tile_hbm, tile_ref), (near_hbm, near_ref))
        )
    ]
    for copy in small:
        copy.start()
    for g in range(groups):
        copy_of(g, jacobi_hbm, jacobi_ref, jacobi_sem).start()
    for g in range(groups):
        copy_of(g, coupling_hbm, coupling_ref, coupling_sem).start()
        copy_of(g, diagonal_hbm, diagonal_ref, diagonal_sem).start()
    for copy in small:
        copy.wait()
    own = lax.axis_index("rows")
    part, tile, near = part_ref[...], tile_ref[...], near_ref[...]
    near_row = lax.broadcasted_iota(jnp.int32, near.shape, 0)
    mine = jnp.sum(jnp.where(near_row == own, near, 0), axis=0, keepdims=True)
    target = jnp.where(part == 0, own, 0)
    for n in range(near.shape[1]):
        target = target + jnp.where(part == n + 1, mine[:, n : n + 1], 0)
    landing = target * (rows * n_sub) + tile
    landing = jnp.concatenate([landing[k : k + 1] for k in range(slots)] * 3, axis=1)
    at = lax.broadcasted_iota(jnp.int32, (spread_ref.shape[0], 1), 0)
    device, line = at // (rows + 1), at % (rows + 1)
    row, sub = device // (n_cols * n_sub), device % n_sub
    wanted = jnp.where(line < rows, row * (rows * n_sub) + sub * rows + line, -1)
    spread_ref[...] = jnp.where(landing == wanted, 1.0, 0.0).astype(jnp.bfloat16)
    m = lax.broadcasted_iota(jnp.int32, (1, 8, width), 1)
    j = lax.broadcasted_iota(jnp.int32, (1, 8, width), 2)
    last = width // BLOCK * BLOCK
    for g in range(groups):
        copy_of(g, jacobi_hbm, jacobi_ref, jacobi_sem).wait()
        folded = jnp.sum(some(jacobi_ref, g)[...].reshape(8, width // 8, 8, width), axis=1)
        for d in range(-BAND, BAND + 1):
            i = j + d
            inside = (i // BLOCK == j // BLOCK) & (j < last) if d else j >= 0
            picked = inside & (i >= 0) & (lax.rem(i + 8, 8) == m)
            band_ref[d + BAND, pl.ds(g * 8, 8)] = jnp.sum(jnp.where(picked, folded, 0.0), axis=1)
    z = apply_m(band_ref, b_ref[...])

    def before(g):
        copy_of(g, coupling_hbm, coupling_ref, coupling_sem).wait()
        copy_of(g, diagonal_hbm, diagonal_ref, diagonal_sem).wait()

    tail = jnp.zeros((1, width), jnp.float32)
    emit(z, tail, spread_ref, coupling_ref, diagonal_ref, (partial_ref, column_ref), own_ref, send_ref, before)


def second_kernel(
    recv_ref, own_in, b_ref, band_ref, spread_ref, coupling_ref, diagonal_ref,
    send_ref, own_ref, q_ref, partial_ref, column_ref,
):
    b = b_ref[...]
    rows, width = b.shape
    q = own_in[...]
    for d in range(recv_ref.shape[0] // (rows + 1)):
        q = q + chunk(recv_ref, d, rows)
    q_ref[...] = q
    up, down = level(q, b)
    tail = pack([total(b * b), total(b * q), down], width)
    z = apply_m(band_ref, q * up)
    emit(z, tail, spread_ref, coupling_ref, diagonal_ref, (partial_ref, column_ref), own_ref, send_ref)


def scalars_of(recv_ref, rows, count, repeats):
    tails = gather_tails(recv_ref, rows)
    summed = functools.reduce(jnp.add, tails)
    return tails, [summed[:, n : n + 1] / repeats for n in range(count)]


def weighted(recv_ref, own_in, own_down, tails, at, factor):
    rows = own_in.shape[0]
    out = own_in[...] * (factor * own_down)
    for d, tail in enumerate(tails):
        out = out + chunk(recv_ref, d, rows) * (factor * tail[:, at : at + 1])
    return out


def third_kernel(
    recv_ref, own_in, b_ref, q_ref, band_ref, spread_ref, coupling_ref, diagonal_ref,
    send_ref, own_ref, twice_ref, half_ref, u_ref, keep_ref, partial_ref, column_ref, *, n_cols,
):
    b, q = b_ref[...], q_ref[...]
    rows, width = b.shape
    tails, (rho, cross) = scalars_of(recv_ref, rows, 2, n_cols)
    alpha = rho / cross
    _, down = level(q, b)
    u = weighted(recv_ref, own_in, down, tails, 2, alpha)
    twice = q - u
    half = b - alpha * q
    up, down = level(twice, half)
    tail = pack([total(twice * half), total(twice * twice), total(b * half), total(b * twice), down], width)
    twice_ref[...], half_ref[...], u_ref[...] = twice, half, u
    keep_ref[...] = pack([rho, alpha], width)
    z = apply_m(band_ref, twice * up)
    emit(z, tail, spread_ref, coupling_ref, diagonal_ref, (partial_ref, column_ref), own_ref, send_ref)


def fourth_kernel(
    recv_ref, own_in, b_ref, q_ref, twice_ref, half_ref, u_ref, keep_ref, band_ref, spread_ref, coupling_ref,
    diagonal_ref, send_ref, own_ref, a_ref, residual_ref, image_ref, search_ref, done_ref, kept_ref, partial_ref, column_ref,
    *, n_cols,
):
    b, q, twice, half = b_ref[...], q_ref[...], twice_ref[...], half_ref[...]
    rows, width = b.shape
    rho, alpha = keep_ref[:, 0:1], keep_ref[:, 1:2]
    tails, (cross, square, b_half, b_twice) = scalars_of(recv_ref, rows, 4, n_cols)
    omega = cross / square
    rho_next = b_half - omega * b_twice
    ratio = rho_next / rho
    beta = ratio * (alpha / omega)
    _, down = level(twice, half)
    a = twice - weighted(recv_ref, own_in, down, tails, 4, omega)
    residual = half - omega * twice
    image = a + beta * q - ratio * u_ref[...]
    up, down = level(image, residual)
    tail = pack([total(b * image), down], width)
    a_ref[...], residual_ref[...], image_ref[...] = a, residual, image
    search_ref[...] = residual + beta * (b - omega * q)
    done_ref[...] = alpha * b + omega * half
    kept_ref[...] = pack([rho_next], width)
    z = apply_m(band_ref, image * up)
    emit(z, tail, spread_ref, coupling_ref, diagonal_ref, (partial_ref, column_ref), own_ref, send_ref)


def fifth_kernel(
    recv_ref, own_in, a_ref, residual_ref, image_ref, search_ref, done_ref, kept_ref,
    twice_ref, half_ref, sum_ref, dots_ref, *, n_cols,
):
    residual, image = residual_ref[...], image_ref[...]
    rows, width = residual.shape
    tails, (cross,) = scalars_of(recv_ref, rows, 1, n_cols)
    alpha = kept_ref[:, 0:1] / cross
    _, down = level(image, residual)
    twice = a_ref[...] - weighted(recv_ref, own_in, down, tails, 1, alpha)
    half = residual - alpha * image
    twice_ref[...], half_ref[...] = twice, half
    sum_ref[...] = done_ref[...] + alpha * search_ref[...]
    dots_ref[...] = pack([total(twice * half), total(twice * twice)], width)


def last_kernel(dots_ref, twice_ref, half_ref, sum_ref, band_ref, solution_ref, residual_ref):
    dots = dots_ref[...]
    omega = dots[:, 0:1] / dots[:, 1:2]
    half = half_ref[...]
    residual_ref[...] = half - omega * twice_ref[...]
    solution_ref[...] = apply_m(band_ref, sum_ref[...] + omega * half)


def partners(count, step):
    if count & (count - 1) == 0:
        return [(i, i ^ step) for i in range(count)]
    return [(i, (i + step) % count) for i in range(count)]


def sum_over(x, axis):
    count = lax.axis_size(axis)
    out = x
    for step in range(1, count):
        out = out + lax.ppermute(x, axis, partners(count, step))
    return out


def call(kernel, outs, args, scratch=(), space=pltpu.VMEM):
    spec = pl.BlockSpec(memory_space=pltpu.VMEM)
    if space == pltpu.HBM:
        args = [pltpu.with_memory_space_constraint(x, space) for x in args]
    return pl.pallas_call(
        kernel,
        out_shape=[pltpu.VMEM(shape, kind) if space == pltpu.HBM else jax.ShapeDtypeStruct(shape, kind) for shape, kind in outs],
        in_specs=[pl.BlockSpec(memory_space=space)] * len(args),
        out_specs=[spec] * len(outs),
        scratch_shapes=list(scratch),
        compiler_params=pltpu.CompilerParams(vmem_limit_bytes=24 << 20),
    )(*args)


def on_device(diagonal, coupling, column_part, column_tile, neighbours, b, jacobi):
    f32 = jnp.float32
    rows, width = b.shape
    slots = coupling.shape[1]
    sizes = tuple(lax.axis_size(axis) for axis in PART)
    n_cols = sizes[1]
    devices = sizes[0] * sizes[1] * sizes[2]
    vec, line = ((rows, width), f32), ((1, width), f32)
    message = ((devices * (rows + 1), width), f32)
    band_shape = ((2 * BAND + 1, rows, width), f32)
    spread_shape = ((devices * (rows + 1), 3 * slots * rows), jnp.bfloat16)
    scratch = [pltpu.VMEM((slots * rows, width), f32), pltpu.VMEM((rows, width, width), f32)]

    def exchange(send):
        send = send.reshape(devices, rows + 1, 1, width)
        return lax.all_to_all(send, PART, 0, 0, tiled=True).reshape(devices * (rows + 1), width)

    part, tile = column_part.T, column_tile.T
    sems = [pltpu.SemaphoreType.DMA((n,)) for n in (4, rows // 8, rows // 8, rows // 8)]
    send, own, band, spread, b, coupling, diagonal = call(
        functools.partial(first_kernel, sizes=sizes),
        [message, vec, band_shape, spread_shape, vec, (coupling.shape, f32), (diagonal.shape, f32)],
        (b, jacobi, part, tile, neighbours, coupling, diagonal),
        scratch
        + [pltpu.VMEM(jacobi.shape, f32)]
        + [pltpu.VMEM(x.shape, x.dtype) for x in (part, tile, neighbours)]
        + sems,
        pltpu.HBM,
    )
    fixed = (band, spread, coupling, diagonal)
    send, own, q = call(second_kernel, [message, vec, vec], (exchange(send), own, b) + fixed, scratch)
    send, own, twice, half, u, keep = call(
        functools.partial(third_kernel, n_cols=n_cols), [message] + [vec] * 4 + [line],
        (exchange(send), own, b, q) + fixed, scratch,
    )
    send, own, a, residual, image, search, done, kept = call(
        functools.partial(fourth_kernel, n_cols=n_cols), [message] + [vec] * 6 + [line],
        (exchange(send), own, b, q, twice, half, u, keep) + fixed, scratch,
    )
    twice, half, summed, dots = call(
        functools.partial(fifth_kernel, n_cols=n_cols), [vec] * 3 + [line],
        (exchange(send), own, a, residual, image, search, done, kept),
    )
    dots = sum_over(sum_over(dots, "sub"), "rows")
    return tuple(call(last_kernel, [vec, vec], (dots, twice, half, summed, band)))


def solution(mesh):
    lines = P(("groups", "rows", "sub"), None)
    tiles = P(("groups", "rows", "sub"), None, None)
    slots = P(("groups", "rows", "sub"), "cols")
    in_specs = (
        tiles, P(("groups", "rows", "sub"), "cols", None, None), slots, slots, P("groups", None), lines, tiles,
    )
    return jax.shard_map(on_device, mesh=mesh, in_specs=in_specs, out_specs=(lines, lines), check_vma=False)
```

```python
import functools

import jax
import jax.numpy as jnp
from jax import lax
from jax.experimental import pallas as pl
from jax.experimental.pallas import tpu as pltpu
from jax.sharding import PartitionSpec as P

BLOCK = 5
BAND = BLOCK - 1
LANES = 128
PART = ("rows", "cols", "sub")


def apply_m(band_ref, v):
    width = v.shape[1]
    z = band_ref[BAND] * v
    for d in range(-BAND, BAND + 1):
        if d:
            z = z + band_ref[d + BAND] * pltpu.roll(v, (-d) % width, 1)
    return z


def split3(x):
    hi = x.astype(jnp.bfloat16)
    rest = x - hi.astype(jnp.float32)
    mid = rest.astype(jnp.bfloat16)
    low = (rest - mid.astype(jnp.float32)).astype(jnp.bfloat16)
    return jnp.concatenate([hi, mid, low], axis=0)


def sum_lines(parts):
    line = lax.broadcasted_iota(jnp.int32, parts[0].shape, 0)
    step = 1
    while len(parts) > 1:
        low = (line // step) % 2 == 0
        parts = [
            jnp.where(low, one, two) + pltpu.roll(jnp.where(low, two, one), step, 0)
            for one, two in zip(parts[::2], parts[1::2])
        ]
        step *= 2
    return parts[0]


def products(z, coupling_ref, diagonal_ref, partial_ref, own_ref, before=None):
    rows, slots, width = coupling_ref.shape[:3]
    for g in range(rows // 8):
        if before is not None:
            before(g)
        first = g * 8
        sums = [[] for _ in range(slots + 1)]
        for r in range(first, first + 8):
            column = jnp.broadcast_to(z[r : r + 1], (width, width)).T
            for k in range(slots):
                sums[k].append(jnp.sum((column * coupling_ref[r, k]).reshape(width // 8, 8, width), axis=0))
            sums[slots].append(jnp.sum((column * diagonal_ref[r]).reshape(width // 8, 8, width), axis=0))
        for k in range(slots):
            partial_ref[pl.ds(k * rows + first, 8), :] = sum_lines(sums[k])
        own_ref[pl.ds(first, 8), :] = sum_lines(sums[slots])


def emit(z, tail, spread_ref, coupling_ref, diagonal_ref, partial_ref, own_ref, send_ref, before=None):
    rows = z.shape[0]
    products(z, coupling_ref, diagonal_ref, partial_ref, own_ref, before)
    send_ref[...] = jnp.dot(spread_ref[...], split3(partial_ref[...]), preferred_element_type=jnp.float32)
    for d in range(send_ref.shape[0] // (rows + 1)):
        send_ref[pl.ds(d * (rows + 1) + rows, 1), :] = tail


def pack(scalars, width):
    lane = lax.broadcasted_iota(jnp.int32, (1, width), 1)
    tail = jnp.zeros((1, width), jnp.float32)
    for at, value in enumerate(scalars):
        tail = jnp.where(lane == at, value, tail)
    return tail


def total(x):
    return jnp.sum(jnp.sum(x, axis=0, keepdims=True), axis=1, keepdims=True)


def peak(x):
    return jnp.max(jnp.max(jnp.abs(x), axis=0, keepdims=True), axis=1, keepdims=True)


def level(x, like):
    size, aim = peak(x), peak(like)
    good = (size > 0) & (aim > 0)
    return jnp.where(good, aim / size, 1.0), jnp.where(good, size / aim, 1.0)


def gather_tails(recv_ref, rows):
    count = recv_ref.shape[0] // (rows + 1)
    return [recv_ref[pl.ds(d * (rows + 1) + rows, 1), :] for d in range(count)]


def chunk(recv_ref, d, rows):
    return recv_ref[pl.ds(d * (rows + 1), rows), :]


def first_kernel(
    b_hbm, jacobi_hbm, part_hbm, tile_hbm, near_hbm, coupling_hbm, diagonal_hbm,
    send_ref, own_ref, band_ref, spread_ref, halves_ref, b_ref, coupling_ref, diagonal_ref,
    partial_ref, jacobi_ref, part_ref, tile_ref, near_ref, small_sem, jacobi_sem, coupling_sem, diagonal_sem,
    *, sizes,
):
    n_rows, n_cols, n_sub = sizes
    rows, slots = coupling_ref.shape[0], coupling_ref.shape[1]
    width = b_ref.shape[1]
    groups = rows // 8

    def some(ref, g):
        return ref.at[pl.ds(g * 8, 8)]

    def copy_of(g, source, target, sem):
        return pltpu.make_async_copy(some(source, g), some(target, g), sem.at[g])

    small = [
        pltpu.make_async_copy(source, target, small_sem.at[n])
        for n, (source, target) in enumerate(
            ((b_hbm, b_ref), (part_hbm, part_ref), (tile_hbm, tile_ref), (near_hbm, near_ref))
        )
    ]
    for copy in small:
        copy.start()
    for g in range(groups):
        copy_of(g, jacobi_hbm, jacobi_ref, jacobi_sem).start()
    for g in range(groups):
        copy_of(g, coupling_hbm, coupling_ref, coupling_sem).start()
        copy_of(g, diagonal_hbm, diagonal_ref, diagonal_sem).start()
    for copy in small:
        copy.wait()
    own = lax.axis_index("rows")
    part, tile, near = part_ref[...], tile_ref[...], near_ref[...]
    near_row = lax.broadcasted_iota(jnp.int32, near.shape, 0)
    mine = jnp.sum(jnp.where(near_row == own, near, 0), axis=0, keepdims=True)
    target = jnp.where(part == 0, own, 0)
    for n in range(near.shape[1]):
        target = target + jnp.where(part == n + 1, mine[:, n : n + 1], 0)
    landing = target * (rows * n_sub) + tile
    landing = jnp.concatenate([landing[k : k + 1] for k in range(slots)] * 3, axis=1)
    at = lax.broadcasted_iota(jnp.int32, (spread_ref.shape[0], 1), 0)
    device, line = at // (rows + 1), at % (rows + 1)
    row, sub = device // (n_cols * n_sub), device % n_sub
    wanted = jnp.where(line < rows, row * (rows * n_sub) + sub * rows + line, -1)
    spread_ref[...] = jnp.where(landing == wanted, 1.0, 0.0).astype(jnp.bfloat16)
    at = lax.broadcasted_iota(jnp.int32, (halves_ref.shape[0], 1), 0)
    size = halves_ref.shape[0] // n_sub
    sub, at = partner(lax.axis_index("sub"), at // size, n_sub), at % size
    wanted = jnp.where(at < n_rows * rows, at // rows * (rows * n_sub) + sub * rows + at % rows, -1)
    halves_ref[...] = jnp.where(landing == wanted, 1.0, 0.0).astype(jnp.bfloat16)
    m = lax.broadcasted_iota(jnp.int32, (1, 8, width), 1)
    j = lax.broadcasted_iota(jnp.int32, (1, 8, width), 2)
    last = width // BLOCK * BLOCK
    for g in range(groups):
        copy_of(g, jacobi_hbm, jacobi_ref, jacobi_sem).wait()
        folded = jnp.sum(some(jacobi_ref, g)[...].reshape(8, width // 8, 8, width), axis=1)
        for d in range(-BAND, BAND + 1):
            i = j + d
            inside = (i // BLOCK == j // BLOCK) & (j < last) if d else j >= 0
            picked = inside & (i >= 0) & (lax.rem(i + 8, 8) == m)
            band_ref[d + BAND, pl.ds(g * 8, 8)] = jnp.sum(jnp.where(picked, folded, 0.0), axis=1)
    z = apply_m(band_ref, b_ref[...])

    def before(g):
        copy_of(g, coupling_hbm, coupling_ref, coupling_sem).wait()
        copy_of(g, diagonal_hbm, diagonal_ref, diagonal_sem).wait()

    tail = jnp.zeros((1, width), jnp.float32)
    emit(z, tail, spread_ref, coupling_ref, diagonal_ref, partial_ref, own_ref, send_ref, before)


def second_kernel(
    recv_ref, own_in, b_ref, band_ref, spread_ref, coupling_ref, diagonal_ref,
    send_ref, own_ref, q_ref, partial_ref,
):
    b = b_ref[...]
    rows, width = b.shape
    q = own_in[...]
    for d in range(recv_ref.shape[0] // (rows + 1)):
        q = q + chunk(recv_ref, d, rows)
    q_ref[...] = q
    up, down = level(q, b)
    tail = pack([total(b * b), total(b * q), down], width)
    z = apply_m(band_ref, q * up)
    emit(z, tail, spread_ref, coupling_ref, diagonal_ref, partial_ref, own_ref, send_ref)


def scalars_of(recv_ref, rows, count, repeats):
    tails = gather_tails(recv_ref, rows)
    summed = functools.reduce(jnp.add, tails)
    return tails, [summed[:, n : n + 1] / repeats for n in range(count)]


def weighted(recv_ref, own_in, own_down, tails, at, factor):
    rows = own_in.shape[0]
    out = own_in[...] * (factor * own_down)
    for d, tail in enumerate(tails):
        out = out + chunk(recv_ref, d, rows) * (factor * tail[:, at : at + 1])
    return out


def third_kernel(
    recv_ref, own_in, b_ref, q_ref, band_ref, spread_ref, coupling_ref, diagonal_ref,
    send_ref, own_ref, twice_ref, half_ref, u_ref, keep_ref, partial_ref, *, n_cols,
):
    b, q = b_ref[...], q_ref[...]
    rows, width = b.shape
    tails, (rho, cross) = scalars_of(recv_ref, rows, 2, n_cols)
    alpha = rho / cross
    _, down = level(q, b)
    u = weighted(recv_ref, own_in, down, tails, 2, alpha)
    twice = q - u
    half = b - alpha * q
    tail = pack([total(twice * half), total(twice * twice), total(b * half), total(b * twice)], width)
    twice_ref[...], half_ref[...], u_ref[...] = twice, half, u
    keep_ref[...] = pack([rho, alpha], width)
    z = apply_m(band_ref, alpha * twice)
    emit(z, tail, spread_ref, coupling_ref, diagonal_ref, partial_ref, own_ref, send_ref)


def fourth_kernel(
    recv_ref, own_in, b_ref, q_ref, twice_ref, half_ref, u_ref, keep_ref, band_ref, halves_ref, coupling_ref,
    diagonal_ref, *refs, n_rows, n_cols, n_sub,
):
    parts, (three_ref, search_ref, done_ref, kept_ref, partial_ref, own_ref) = refs[:n_sub], refs[n_sub:]
    b, q, twice, half = b_ref[...], q_ref[...], twice_ref[...], half_ref[...]
    rows, width = b.shape
    rho, alpha = keep_ref[:, 0:1], keep_ref[:, 1:2]
    _, (cross, square, b_half, b_twice) = scalars_of(recv_ref, rows, 4, n_cols)
    omega = cross / square
    rho_next = b_half - omega * b_twice
    ratio = rho_next / rho
    beta = ratio * (alpha / omega)
    a = own_in[...]
    for d in range(recv_ref.shape[0] // (rows + 1)):
        a = a + chunk(recv_ref, d, rows)
    a = twice - (omega / alpha) * a
    residual = half - omega * twice
    image = a + beta * q - ratio * u_ref[...]
    three_ref[...] = jnp.concatenate([a, residual, image], axis=0)
    search_ref[...] = residual + beta * (b - omega * q)
    done_ref[...] = alpha * b + omega * half
    kept_ref[...] = pack([rho_next, alpha], width)
    first = lax.axis_index("cols") == 0
    tail = pack([jnp.where(first, total(b * image), 0.0)], width)
    z = apply_m(band_ref, alpha * image)
    products(z, coupling_ref, diagonal_ref, partial_ref, own_ref)
    out = jnp.dot(halves_ref[...], split3(partial_ref[...]), preferred_element_type=jnp.float32)
    size = parts[0].shape[0]
    for t, part_ref in enumerate(parts):
        part_ref[...] = out[t * size : (t + 1) * size]
        part_ref[pl.ds(n_rows * rows, 1), :] = tail
    here = pl.ds(pl.multiple_of(lax.axis_index("rows") * rows, rows), rows)
    parts[0][here, :] = parts[0][here, :] + jnp.where(first, own_ref[...], 0.0)


def fifth_kernel(mine_ref, *refs, n_rows):
    others, (kept_ref, search_ref, done_ref, twice_ref, half_ref, sum_ref, dots_ref, full_ref) = (
        refs[: n_rows - 1],
        refs[n_rows - 1 :],
    )
    rows, width = search_ref.shape
    size = full_ref.shape[0]
    full = mine_ref[pl.ds(0, size), :]
    for other in others:
        full = full + other[pl.ds(0, size), :]
    full_ref[...] = full
    tail = full[n_rows * rows : n_rows * rows + 1]
    alpha = kept_ref[:, 0:1] / tail[:, 0:1]
    factor = alpha / kept_ref[:, 1:2]
    own = lax.axis_index("rows")
    cross = square = None
    for step, source in enumerate((mine_ref,) + tuple(others)):
        at = own if step == 0 else sender(own, step, n_rows)
        a, residual, image = (source[pl.ds(size + n * rows, rows), :] for n in range(3))
        twice = a - factor * full_ref[pl.ds(pl.multiple_of(at * rows, rows), rows), :]
        half = residual - alpha * image
        if step == 0:
            twice_ref[...], half_ref[...] = twice, half
            cross, square = twice * half, twice * twice
        else:
            cross, square = cross + twice * half, square + twice * twice
    sum_ref[...] = done_ref[...] + alpha * search_ref[...]
    dots_ref[...] = pack([total(cross), total(square)], width)


def last_kernel(dots_ref, twice_ref, half_ref, sum_ref, band_ref, solution_ref, residual_ref):
    dots = dots_ref[...]
    omega = dots[:, 0:1] / dots[:, 1:2]
    half = half_ref[...]
    residual_ref[...] = half - omega * twice_ref[...]
    solution_ref[...] = apply_m(band_ref, sum_ref[...] + omega * half)


def partner(at, step, count):
    return at ^ step if count & (count - 1) == 0 else (at + step) % count


def sender(at, step, count):
    return at ^ step if count & (count - 1) == 0 else (at + count - step) % count


def shifted(x, axis, step):
    count = lax.axis_size(axis)
    return lax.ppermute(x, axis, [(i, partner(i, step, count)) for i in range(count)])


def sum_over(x, axis):
    out = x
    for step in range(1, lax.axis_size(axis)):
        out = out + shifted(x, axis, step)
    return out


def call(kernel, outs, args, scratch=(), space=pltpu.VMEM):
    spec = pl.BlockSpec(memory_space=pltpu.VMEM)
    if space == pltpu.HBM:
        args = [pltpu.with_memory_space_constraint(x, space) for x in args]
    return pl.pallas_call(
        kernel,
        out_shape=[pltpu.VMEM(shape, kind) if space == pltpu.HBM else jax.ShapeDtypeStruct(shape, kind) for shape, kind in outs],
        in_specs=[pl.BlockSpec(memory_space=space)] * len(args),
        out_specs=[spec] * len(outs),
        scratch_shapes=list(scratch),
        compiler_params=pltpu.CompilerParams(vmem_limit_bytes=24 << 20),
    )(*args)


def on_device(diagonal, coupling, column_part, column_tile, neighbours, b, jacobi):
    f32 = jnp.float32
    rows, width = b.shape
    slots = coupling.shape[1]
    sizes = tuple(lax.axis_size(axis) for axis in PART)
    n_rows, n_cols, n_sub = sizes
    devices = n_rows * n_cols * n_sub
    vec, line = ((rows, width), f32), ((1, width), f32)
    message = ((devices * (rows + 1), width), f32)
    part_size = n_rows * rows + 8
    part_shape = ((part_size, width), f32)
    band_shape = ((2 * BAND + 1, rows, width), f32)
    spread_shape = ((devices * (rows + 1), 3 * slots * rows), jnp.bfloat16)
    halves_shape = ((n_sub * part_size, 3 * slots * rows), jnp.bfloat16)
    scratch = [pltpu.VMEM((slots * rows, width), f32)]

    def exchange(send):
        send = send.reshape(devices, rows + 1, 1, width)
        return lax.all_to_all(send, PART, 0, 0, tiled=True).reshape(devices * (rows + 1), width)

    part, tile = column_part.T, column_tile.T
    sems = [pltpu.SemaphoreType.DMA((n,)) for n in (4, rows // 8, rows // 8, rows // 8)]
    send, own, band, spread, halves, b, coupling, diagonal = call(
        functools.partial(first_kernel, sizes=sizes),
        [message, vec, band_shape, spread_shape, halves_shape, vec, (coupling.shape, f32), (diagonal.shape, f32)],
        (b, jacobi, part, tile, neighbours, coupling, diagonal),
        scratch
        + [pltpu.VMEM(jacobi.shape, f32)]
        + [pltpu.VMEM(x.shape, x.dtype) for x in (part, tile, neighbours)]
        + sems,
        pltpu.HBM,
    )
    tiles = (coupling, diagonal)
    send, own, q = call(
        second_kernel, [message, vec, vec], (exchange(send), own, b, band, spread) + tiles, scratch
    )
    send, own, twice, half, u, keep = call(
        functools.partial(third_kernel, n_cols=n_cols), [message] + [vec] * 4 + [line],
        (exchange(send), own, b, q, band, spread) + tiles, scratch,
    )
    *parts, three, search, done, kept = call(
        functools.partial(fourth_kernel, n_rows=n_rows, n_cols=n_cols, n_sub=n_sub),
        [part_shape] * n_sub + [((3 * rows, width), f32), vec, vec, line],
        (exchange(send), own, b, q, twice, half, u, keep, band, halves) + tiles,
        scratch + [pltpu.VMEM((rows, width), f32)],
    )
    summed = parts[0]
    for step in range(1, n_sub):
        summed = summed + shifted(parts[step], "sub", step)
    summed = sum_over(summed, "cols")
    mine = jnp.concatenate([summed, three])
    others = [shifted(mine, "rows", step) for step in range(1, n_rows)]
    twice, half, total_search, dots = call(
        functools.partial(fifth_kernel, n_rows=n_rows), [vec] * 3 + [line],
        (mine, *others, kept, search, done), [pltpu.VMEM((part_size, width), f32)],
    )
    dots = sum_over(dots, "sub")
    return tuple(call(last_kernel, [vec, vec], (dots, twice, half, total_search, band)))


def solution(mesh):
    lines = P(("groups", "rows", "sub"), None)
    tiles = P(("groups", "rows", "sub"), None, None)
    slots = P(("groups", "rows", "sub"), "cols")
    in_specs = (
        tiles, P(("groups", "rows", "sub"), "cols", None, None), slots, slots, P("groups", None), lines, tiles,
    )
    return jax.shard_map(on_device, mesh=mesh, in_specs=in_specs, out_specs=(lines, lines), check_vma=False)
```

```python
import functools

import jax
import jax.numpy as jnp
from jax import lax
from jax.experimental import pallas as pl
from jax.experimental.pallas import tpu as pltpu
from jax.sharding import PartitionSpec as P

BLOCK = 5
BAND = BLOCK - 1
LANES = 128
PART = ("rows", "cols", "sub")


def apply_m(band_ref, v):
    width = v.shape[1]
    z = band_ref[BAND] * v
    for d in range(-BAND, BAND + 1):
        if d:
            z = z + band_ref[d + BAND] * pltpu.roll(v, (-d) % width, 1)
    return z


def split3(x):
    hi = x.astype(jnp.bfloat16)
    rest = x - hi.astype(jnp.float32)
    mid = rest.astype(jnp.bfloat16)
    low = (rest - mid.astype(jnp.float32)).astype(jnp.bfloat16)
    return jnp.concatenate([hi, mid, low], axis=0)


def sum_lines(parts):
    line = lax.broadcasted_iota(jnp.int32, parts[0].shape, 0)
    step = 1
    while len(parts) > 1:
        low = (line // step) % 2 == 0
        parts = [
            jnp.where(low, one, two) + pltpu.roll(jnp.where(low, two, one), step, 0)
            for one, two in zip(parts[::2], parts[1::2])
        ]
        step *= 2
    return parts[0]


def products(z, coupling_ref, diagonal_ref, partial_ref, own_ref, before=None):
    rows, slots, width = coupling_ref.shape[:3]
    for g in range(rows // 8):
        if before is not None:
            before(g)
        first = g * 8
        sums = [[] for _ in range(slots + 1)]
        for r in range(first, first + 8):
            column = jnp.broadcast_to(z[r : r + 1], (width, width)).T
            for k in range(slots):
                sums[k].append(jnp.sum((column * coupling_ref[r, k]).reshape(width // 8, 8, width), axis=0))
            sums[slots].append(jnp.sum((column * diagonal_ref[r]).reshape(width // 8, 8, width), axis=0))
        for k in range(slots):
            partial_ref[pl.ds(k * rows + first, 8), :] = sum_lines(sums[k])
        own_ref[pl.ds(first, 8), :] = sum_lines(sums[slots])


def emit(z, tail, spread_ref, coupling_ref, diagonal_ref, partial_ref, own_ref, send_ref, before=None):
    rows = z.shape[0]
    products(z, coupling_ref, diagonal_ref, partial_ref, own_ref, before)
    send_ref[...] = jnp.dot(spread_ref[...], split3(partial_ref[...]), preferred_element_type=jnp.float32)
    for d in range(send_ref.shape[0] // (rows + 1)):
        send_ref[pl.ds(d * (rows + 1) + rows, 1), :] = tail


def pack(scalars, width):
    lane = lax.broadcasted_iota(jnp.int32, (1, width), 1)
    tail = jnp.zeros((1, width), jnp.float32)
    for at, value in enumerate(scalars):
        tail = jnp.where(lane == at, value, tail)
    return tail


def total(x):
    return jnp.sum(jnp.sum(x, axis=0, keepdims=True), axis=1, keepdims=True)


def peak(x):
    return jnp.max(jnp.max(jnp.abs(x), axis=0, keepdims=True), axis=1, keepdims=True)


def level(x, like):
    size, aim = peak(x), peak(like)
    good = (size > 0) & (aim > 0)
    return jnp.where(good, aim / size, 1.0), jnp.where(good, size / aim, 1.0)


def gather_tails(recv_ref, rows):
    count = recv_ref.shape[0] // (rows + 1)
    return [recv_ref[pl.ds(d * (rows + 1) + rows, 1), :] for d in range(count)]


def chunk(recv_ref, d, rows):
    return recv_ref[pl.ds(d * (rows + 1), rows), :]


def first_kernel(
    b_hbm, jacobi_hbm, part_hbm, tile_hbm, near_hbm, coupling_hbm, diagonal_hbm,
    send_ref, own_ref, band_ref, spread_ref, halves_ref, b_ref, coupling_ref, diagonal_ref,
    partial_ref, jacobi_ref, part_ref, tile_ref, near_ref, small_sem, jacobi_sem, coupling_sem, diagonal_sem,
    *, sizes,
):
    n_rows, n_cols, n_sub = sizes
    rows, slots = coupling_ref.shape[0], coupling_ref.shape[1]
    width = b_ref.shape[1]
    groups = rows // 8

    def some(ref, g):
        return ref.at[pl.ds(g * 8, 8)]

    def copy_of(g, source, target, sem):
        return pltpu.make_async_copy(some(source, g), some(target, g), sem.at[g])

    small = [
        pltpu.make_async_copy(source, target, small_sem.at[n])
        for n, (source, target) in enumerate(
            ((b_hbm, b_ref), (part_hbm, part_ref), (tile_hbm, tile_ref), (near_hbm, near_ref))
        )
    ]
    for copy in small:
        copy.start()
    for g in range(groups):
        copy_of(g, jacobi_hbm, jacobi_ref, jacobi_sem).start()
    for g in range(groups):
        copy_of(g, coupling_hbm, coupling_ref, coupling_sem).start()
        copy_of(g, diagonal_hbm, diagonal_ref, diagonal_sem).start()
    for copy in small:
        copy.wait()
    own = lax.axis_index("rows")
    part, tile, near = part_ref[...], tile_ref[...], near_ref[...]
    near_row = lax.broadcasted_iota(jnp.int32, near.shape, 0)
    mine = jnp.sum(jnp.where(near_row == own, near, 0), axis=0, keepdims=True)
    target = jnp.where(part == 0, own, 0)
    for n in range(near.shape[1]):
        target = target + jnp.where(part == n + 1, mine[:, n : n + 1], 0)
    landing = target * (rows * n_sub) + tile
    landing = jnp.concatenate([landing[k : k + 1] for k in range(slots)] * 3, axis=1)
    at = lax.broadcasted_iota(jnp.int32, (spread_ref.shape[0], 1), 0)
    device, line = at // (rows + 1), at % (rows + 1)
    row, sub = device // (n_cols * n_sub), device % n_sub
    wanted = jnp.where(line < rows, row * (rows * n_sub) + sub * rows + line, -1)
    spread_ref[...] = jnp.where(landing == wanted, 1.0, 0.0).astype(jnp.bfloat16)
    at = lax.broadcasted_iota(jnp.int32, (halves_ref.shape[0], 1), 0)
    size = halves_ref.shape[0] // n_sub
    sub, at = partner(lax.axis_index("sub"), at // size, n_sub), at % size
    wanted = jnp.where(at < n_rows * rows, at // rows * (rows * n_sub) + sub * rows + at % rows, -1)
    halves_ref[...] = jnp.where(landing == wanted, 1.0, 0.0).astype(jnp.bfloat16)
    m = lax.broadcasted_iota(jnp.int32, (1, 8, width), 1)
    j = lax.broadcasted_iota(jnp.int32, (1, 8, width), 2)
    last = width // BLOCK * BLOCK
    for g in range(groups):
        copy_of(g, jacobi_hbm, jacobi_ref, jacobi_sem).wait()
        folded = jnp.sum(some(jacobi_ref, g)[...].reshape(8, width // 8, 8, width), axis=1)
        for d in range(-BAND, BAND + 1):
            i = j + d
            inside = (i // BLOCK == j // BLOCK) & (j < last) if d else j >= 0
            picked = inside & (i >= 0) & (lax.rem(i + 8, 8) == m)
            band_ref[d + BAND, pl.ds(g * 8, 8)] = jnp.sum(jnp.where(picked, folded, 0.0), axis=1)
    z = apply_m(band_ref, b_ref[...])

    def before(g):
        copy_of(g, coupling_hbm, coupling_ref, coupling_sem).wait()
        copy_of(g, diagonal_hbm, diagonal_ref, diagonal_sem).wait()

    tail = jnp.zeros((1, width), jnp.float32)
    emit(z, tail, spread_ref, coupling_ref, diagonal_ref, partial_ref, own_ref, send_ref, before)


def second_kernel(
    recv_ref, own_in, b_ref, band_ref, spread_ref, coupling_ref, diagonal_ref,
    send_ref, own_ref, q_ref, partial_ref,
):
    b = b_ref[...]
    rows, width = b.shape
    q = own_in[...]
    for d in range(recv_ref.shape[0] // (rows + 1)):
        q = q + chunk(recv_ref, d, rows)
    q_ref[...] = q
    up, down = level(q, b)
    tail = pack([total(b * b), total(b * q), down], width)
    z = apply_m(band_ref, q * up)
    emit(z, tail, spread_ref, coupling_ref, diagonal_ref, partial_ref, own_ref, send_ref)


def scalars_of(recv_ref, rows, count, repeats):
    tails = gather_tails(recv_ref, rows)
    summed = functools.reduce(jnp.add, tails)
    return tails, [summed[:, n : n + 1] / repeats for n in range(count)]


def weighted(recv_ref, own_in, own_down, tails, at, factor):
    rows = own_in.shape[0]
    out = own_in[...] * (factor * own_down)
    for d, tail in enumerate(tails):
        out = out + chunk(recv_ref, d, rows) * (factor * tail[:, at : at + 1])
    return out


def third_kernel(
    recv_ref, own_in, b_ref, q_ref, band_ref, spread_ref, coupling_ref, diagonal_ref,
    send_ref, own_ref, twice_ref, half_ref, u_ref, keep_ref, partial_ref, *, n_cols,
):
    b, q = b_ref[...], q_ref[...]
    rows, width = b.shape
    tails, (rho, cross) = scalars_of(recv_ref, rows, 2, n_cols)
    alpha = rho / cross
    _, down = level(q, b)
    u = weighted(recv_ref, own_in, down, tails, 2, alpha)
    twice = q - u
    half = b - alpha * q
    tail = pack([total(twice * half), total(twice * twice), total(b * half), total(b * twice)], width)
    twice_ref[...], half_ref[...], u_ref[...] = twice, half, u
    keep_ref[...] = pack([rho, alpha], width)
    z = apply_m(band_ref, alpha * twice)
    emit(z, tail, spread_ref, coupling_ref, diagonal_ref, partial_ref, own_ref, send_ref)


def fourth_kernel(
    recv_ref, own_in, b_ref, q_ref, twice_ref, half_ref, u_ref, keep_ref, band_ref, halves_ref, coupling_ref,
    diagonal_ref, *refs, n_rows, n_cols, n_sub,
):
    parts, (three_ref, search_ref, done_ref, kept_ref, partial_ref, own_ref) = refs[:n_sub], refs[n_sub:]
    b, q, twice, half = b_ref[...], q_ref[...], twice_ref[...], half_ref[...]
    rows, width = b.shape
    rho, alpha = keep_ref[:, 0:1], keep_ref[:, 1:2]
    _, (cross, square, b_half, b_twice) = scalars_of(recv_ref, rows, 4, n_cols)
    omega = cross / square
    rho_next = b_half - omega * b_twice
    ratio = rho_next / rho
    beta = ratio * (alpha / omega)
    a = own_in[...]
    for d in range(recv_ref.shape[0] // (rows + 1)):
        a = a + chunk(recv_ref, d, rows)
    a = twice - (omega / alpha) * a
    residual = half - omega * twice
    image = a + beta * q - ratio * u_ref[...]
    three_ref[...] = jnp.concatenate([a, residual, image], axis=0)
    search_ref[...] = residual + beta * (b - omega * q)
    done_ref[...] = alpha * b + omega * half
    kept_ref[...] = pack([rho_next, alpha], width)
    first = lax.axis_index("cols") == 0
    tail = pack([jnp.where(first, total(b * image), 0.0)], width)
    z = apply_m(band_ref, alpha * image)
    products(z, coupling_ref, diagonal_ref, partial_ref, own_ref)
    out = jnp.dot(halves_ref[...], split3(partial_ref[...]), preferred_element_type=jnp.float32)
    size = parts[0].shape[0]
    for t, part_ref in enumerate(parts):
        part_ref[...] = out[t * size : (t + 1) * size]
        part_ref[pl.ds(n_rows * rows, 1), :] = tail
    here = pl.ds(pl.multiple_of(lax.axis_index("rows") * rows, rows), rows)
    parts[0][here, :] = parts[0][here, :] + jnp.where(first, own_ref[...], 0.0)


def fifth_kernel(mine_ref, *refs, order, n_rows):
    others, (kept_ref, search_ref, done_ref, twice_ref, half_ref, sum_ref, dots_ref, full_ref) = (
        refs[: n_rows - 1],
        refs[n_rows - 1 :],
    )
    rows, width = search_ref.shape
    size = full_ref.shape[0]
    full = mine_ref[pl.ds(0, size), :]
    for other in others:
        full = full + other[pl.ds(0, size), :]
    full_ref[...] = full
    tail = full[n_rows * rows : n_rows * rows + 1]
    alpha = kept_ref[:, 0:1] / tail[:, 0:1]
    factor = alpha / kept_ref[:, 1:2]
    own = lax.axis_index("rows")
    cross = square = None
    for step, source in [(0, mine_ref)] + [(n + 1, other) for n, other in zip(order, others)]:
        at = own if step == 0 else sender(own, step, n_rows)
        a, residual, image = (source[pl.ds(size + n * rows, rows), :] for n in range(3))
        twice = a - factor * full_ref[pl.ds(pl.multiple_of(at * rows, rows), rows), :]
        half = residual - alpha * image
        if step == 0:
            twice_ref[...], half_ref[...] = twice, half
            cross, square = twice * half, twice * twice
        else:
            cross, square = cross + twice * half, square + twice * twice
    sum_ref[...] = done_ref[...] + alpha * search_ref[...]
    dots_ref[...] = pack([total(cross), total(square)], width)


def map_kernel(half_ref, sum_ref, band_ref, half_hat_ref, sum_hat_ref):
    half_hat_ref[...] = apply_m(band_ref, half_ref[...])
    sum_hat_ref[...] = apply_m(band_ref, sum_ref[...])


def last_kernel(twice_ref, half_ref, half_hat_ref, sum_hat_ref, *refs):
    *shares, solution_ref, residual_ref = refs
    dots = functools.reduce(jnp.add, [share[...] for share in shares])
    omega = dots[:, 0:1] / dots[:, 1:2]
    residual_ref[...] = half_ref[...] - omega * twice_ref[...]
    solution_ref[...] = sum_hat_ref[...] + omega * half_hat_ref[...]


def partner(at, step, count):
    return at ^ step if count & (count - 1) == 0 else (at + step) % count


def sender(at, step, count):
    return at ^ step if count & (count - 1) == 0 else (at + count - step) % count


def shifted(x, axis, step):
    count = lax.axis_size(axis)
    return lax.ppermute(x, axis, [(i, partner(i, step, count)) for i in range(count)])


def sum_over(x, axis):
    out = x
    for step in range(1, lax.axis_size(axis)):
        out = out + shifted(x, axis, step)
    return out


def call(kernel, outs, args, scratch=(), space=pltpu.VMEM):
    spec = pl.BlockSpec(memory_space=pltpu.VMEM)
    if space == pltpu.HBM:
        args = [pltpu.with_memory_space_constraint(x, space) for x in args]
    return pl.pallas_call(
        kernel,
        out_shape=[pltpu.VMEM(shape, kind) if space == pltpu.HBM else jax.ShapeDtypeStruct(shape, kind) for shape, kind in outs],
        in_specs=[pl.BlockSpec(memory_space=space)] * len(args),
        out_specs=[spec] * len(outs),
        scratch_shapes=list(scratch),
        compiler_params=pltpu.CompilerParams(vmem_limit_bytes=24 << 20),
    )(*args)


def on_device(diagonal, coupling, column_part, column_tile, neighbours, b, jacobi):
    f32 = jnp.float32
    rows, width = b.shape
    slots = coupling.shape[1]
    sizes = tuple(lax.axis_size(axis) for axis in PART)
    n_rows, n_cols, n_sub = sizes
    devices = n_rows * n_cols * n_sub
    vec, line = ((rows, width), f32), ((1, width), f32)
    message = ((devices * (rows + 1), width), f32)
    part_size = n_rows * rows + 8
    part_shape = ((part_size, width), f32)
    band_shape = ((2 * BAND + 1, rows, width), f32)
    spread_shape = ((devices * (rows + 1), 3 * slots * rows), jnp.bfloat16)
    halves_shape = ((n_sub * part_size, 3 * slots * rows), jnp.bfloat16)
    scratch = [pltpu.VMEM((slots * rows, width), f32)]

    def exchange(send):
        send = send.reshape(devices, rows + 1, 1, width)
        return lax.all_to_all(send, PART, 0, 0, tiled=True).reshape(devices * (rows + 1), width)

    part, tile = column_part.T, column_tile.T
    sems = [pltpu.SemaphoreType.DMA((n,)) for n in (4, rows // 8, rows // 8, rows // 8)]
    send, own, band, spread, halves, b, coupling, diagonal = call(
        functools.partial(first_kernel, sizes=sizes),
        [message, vec, band_shape, spread_shape, halves_shape, vec, (coupling.shape, f32), (diagonal.shape, f32)],
        (b, jacobi, part, tile, neighbours, coupling, diagonal),
        scratch
        + [pltpu.VMEM(jacobi.shape, f32)]
        + [pltpu.VMEM(x.shape, x.dtype) for x in (part, tile, neighbours)]
        + sems,
        pltpu.HBM,
    )
    tiles = (coupling, diagonal)
    send, own, q = call(
        second_kernel, [message, vec, vec], (exchange(send), own, b, band, spread) + tiles, scratch
    )
    send, own, twice, half, u, keep = call(
        functools.partial(third_kernel, n_cols=n_cols), [message] + [vec] * 4 + [line],
        (exchange(send), own, b, q, band, spread) + tiles, scratch,
    )
    *parts, three, search, done, kept = call(
        functools.partial(fourth_kernel, n_rows=n_rows, n_cols=n_cols, n_sub=n_sub),
        [part_shape] * n_sub + [((3 * rows, width), f32), vec, vec, line],
        (exchange(send), own, b, q, twice, half, u, keep, band, halves) + tiles,
        scratch + [pltpu.VMEM((rows, width), f32)],
    )
    summed = parts[0]
    for step in range(1, n_sub):
        summed = summed + shifted(parts[step], "sub", step)
    summed = sum_over(summed, "cols")
    mine = jnp.concatenate([summed, three])
    others = [shifted(mine, "rows", step) for step in range(1, n_rows)]
    order = [1, 0, *range(2, n_rows - 1)]
    twice, half, total_search, dots = call(
        functools.partial(fifth_kernel, order=order, n_rows=n_rows), [vec] * 3 + [line],
        (mine, *(others[n] for n in order), kept, search, done), [pltpu.VMEM((part_size, width), f32)],
    )
    half_hat, sum_hat = call(map_kernel, [vec, vec], (half, total_search, band))
    shares = [dots] + [shifted(dots, "sub", step) for step in range(1, n_sub)]
    return tuple(call(last_kernel, [vec, vec], (twice, half, half_hat, sum_hat, *shares)))


def solution(mesh):
    lines = P(("groups", "rows", "sub"), None)
    tiles = P(("groups", "rows", "sub"), None, None)
    slots = P(("groups", "rows", "sub"), "cols")
    in_specs = (
        tiles, P(("groups", "rows", "sub"), "cols", None, None), slots, slots, P("groups", None), lines, tiles,
    )
    return jax.shard_map(on_device, mesh=mesh, in_specs=in_specs, out_specs=(lines, lines), check_vma=False)
```

```python
import functools

import jax
import jax.numpy as jnp
from jax import lax
from jax.experimental import pallas as pl
from jax.experimental.pallas import tpu as pltpu
from jax.sharding import PartitionSpec as P

BLOCK = 5
BAND = BLOCK - 1
LANES = 128
PART = ("rows", "sub", "cols")


def apply_m(band_ref, v):
    width = v.shape[1]
    z = band_ref[BAND] * v
    for d in range(-BAND, BAND + 1):
        if d:
            z = z + band_ref[d + BAND] * pltpu.roll(v, (-d) % width, 1)
    return z


def split3(x):
    hi = x.astype(jnp.bfloat16)
    rest = x - hi.astype(jnp.float32)
    mid = rest.astype(jnp.bfloat16)
    low = (rest - mid.astype(jnp.float32)).astype(jnp.bfloat16)
    return jnp.concatenate([hi, mid, low], axis=0)


def sum_lines(parts):
    line = lax.broadcasted_iota(jnp.int32, parts[0].shape, 0)
    step = 1
    while len(parts) > 1:
        low = (line // step) % 2 == 0
        parts = [
            jnp.where(low, one, two) + pltpu.roll(jnp.where(low, two, one), step, 0)
            for one, two in zip(parts[::2], parts[1::2])
        ]
        step *= 2
    return parts[0]


def products(z, coupling_ref, diagonal_ref, partial_ref, own_ref, before=None):
    rows, slots, width = coupling_ref.shape[:3]
    for g in range(rows // 8):
        if before is not None:
            before(g)
        first = g * 8
        sums = [[] for _ in range(slots + 1)]
        for r in range(first, first + 8):
            column = jnp.broadcast_to(z[r : r + 1], (width, width)).T
            for k in range(slots):
                sums[k].append(jnp.sum((column * coupling_ref[r, k]).reshape(width // 8, 8, width), axis=0))
            sums[slots].append(jnp.sum((column * diagonal_ref[r]).reshape(width // 8, 8, width), axis=0))
        for k in range(slots):
            partial_ref[pl.ds(k * rows + first, 8), :] = sum_lines(sums[k])
        own_ref[pl.ds(first, 8), :] = sum_lines(sums[slots])


def emit(z, tail, spread_ref, coupling_ref, diagonal_ref, partial_ref, own_ref, send_ref, before=None):
    rows = z.shape[0]
    products(z, coupling_ref, diagonal_ref, partial_ref, own_ref, before)
    send_ref[...] = jnp.dot(spread_ref[...], split3(partial_ref[...]), preferred_element_type=jnp.float32)
    if callable(tail):
        tail = tail()
    for d in range(send_ref.shape[0] // (rows + 1)):
        send_ref[pl.ds(d * (rows + 1) + rows, 1), :] = tail


def pack(scalars, width):
    lane = lax.broadcasted_iota(jnp.int32, (1, width), 1)
    tail = jnp.zeros((1, width), jnp.float32)
    for at, value in enumerate(scalars):
        tail = jnp.where(lane == at, value, tail)
    return tail


def total(x):
    return jnp.sum(jnp.sum(x, axis=0, keepdims=True), axis=1, keepdims=True)


def peak(x):
    return jnp.max(jnp.max(jnp.abs(x), axis=0, keepdims=True), axis=1, keepdims=True)


def pairwise(join, items):
    items = list(items)
    while len(items) > 1:
        items = [join(*items[n : n + 2]) if n + 1 < len(items) else items[n] for n in range(0, len(items), 2)]
    return items[0]


def tails_of(recv_ref, rows):
    count = recv_ref.shape[0] // (rows + 1)
    return [recv_ref[pl.ds(d * (rows + 1) + rows, 1), :] for d in range(count)]


def chunk(recv_ref, d, rows):
    return recv_ref[pl.ds(d * (rows + 1), rows), :]


def chunks_of(recv_ref, own_in):
    rows = own_in.shape[0]
    return pairwise(jnp.add, [own_in[...]] + [chunk(recv_ref, d, rows) for d in range(recv_ref.shape[0] // (rows + 1))])


def first_kernel(
    b_hbm, jacobi_hbm, part_hbm, tile_hbm, near_hbm, coupling_hbm, diagonal_hbm,
    send_ref, own_ref, band_ref, spread_ref, halves_ref, b_ref, coupling_ref, diagonal_ref,
    partial_ref, jacobi_ref, part_ref, tile_ref, near_ref, small_sem, jacobi_sem, coupling_sem, diagonal_sem,
    *, sizes,
):
    n_rows, n_cols, n_sub = sizes
    rows, slots = coupling_ref.shape[0], coupling_ref.shape[1]
    width = b_ref.shape[1]
    groups = rows // 8

    def some(ref, g):
        return ref.at[pl.ds(g * 8, 8)]

    def copy_of(g, source, target, sem):
        return pltpu.make_async_copy(some(source, g), some(target, g), sem.at[g])

    small = [
        pltpu.make_async_copy(source, target, small_sem.at[n])
        for n, (source, target) in enumerate(
            ((b_hbm, b_ref), (part_hbm, part_ref), (tile_hbm, tile_ref), (near_hbm, near_ref))
        )
    ]
    for copy in small:
        copy.start()
    for g in range(groups):
        copy_of(g, jacobi_hbm, jacobi_ref, jacobi_sem).start()
    for g in range(groups):
        copy_of(g, coupling_hbm, coupling_ref, coupling_sem).start()
        copy_of(g, diagonal_hbm, diagonal_ref, diagonal_sem).start()
    for copy in small:
        copy.wait()
    own = lax.axis_index("rows")
    part, tile, near = part_ref[...], tile_ref[...], near_ref[...]
    near_row = lax.broadcasted_iota(jnp.int32, near.shape, 0)
    mine = jnp.sum(jnp.where(near_row == own, near, 0), axis=0, keepdims=True)
    target = jnp.where(part == 0, own, 0)
    for n in range(near.shape[1]):
        target = target + jnp.where(part == n + 1, mine[:, n : n + 1], 0)
    landing = target * (rows * n_sub) + tile
    landing = jnp.concatenate([landing[k : k + 1] for k in range(slots)] * 3, axis=1)
    at = lax.broadcasted_iota(jnp.int32, (spread_ref.shape[0], 1), 0)
    device, line = at // (rows + 1), at % (rows + 1)
    row, sub = device // (n_cols * n_sub), device // n_cols % n_sub
    wanted = jnp.where(line < rows, row * (rows * n_sub) + sub * rows + line, -1)
    spread_ref[...] = jnp.where(landing == wanted, 1.0, 0.0).astype(jnp.bfloat16)
    at = lax.broadcasted_iota(jnp.int32, (halves_ref.shape[0], 1), 0)
    size = halves_ref.shape[0] // n_sub
    sub, at = partner(lax.axis_index("sub"), at // size, n_sub), at % size
    wanted = jnp.where(at < n_rows * rows, at // rows * (rows * n_sub) + sub * rows + at % rows, -1)
    halves_ref[...] = jnp.where(landing == wanted, 1.0, 0.0).astype(jnp.bfloat16)
    m = lax.broadcasted_iota(jnp.int32, (1, 8, width), 1)
    j = lax.broadcasted_iota(jnp.int32, (1, 8, width), 2)
    last = width // BLOCK * BLOCK
    for g in range(groups):
        copy_of(g, jacobi_hbm, jacobi_ref, jacobi_sem).wait()
        folded = jnp.sum(some(jacobi_ref, g)[...].reshape(8, width // 8, 8, width), axis=1)
        for d in range(-BAND, BAND + 1):
            i = j + d
            inside = (i // BLOCK == j // BLOCK) & (j < last) if d else j >= 0
            picked = inside & (i >= 0) & (lax.rem(i + 8, 8) == m)
            band_ref[d + BAND, pl.ds(g * 8, 8)] = jnp.sum(jnp.where(picked, folded, 0.0), axis=1)
    z = apply_m(band_ref, b_ref[...])

    def before(g):
        copy_of(g, coupling_hbm, coupling_ref, coupling_sem).wait()
        copy_of(g, diagonal_hbm, diagonal_ref, diagonal_sem).wait()

    def tail():
        return pack([peak(b_ref[...]), jnp.maximum(peak(partial_ref[...]), peak(own_ref[...]))], width)

    emit(z, tail, spread_ref, coupling_ref, diagonal_ref, partial_ref, own_ref, send_ref, before)


def second_kernel(
    recv_ref, own_in, b_ref, band_ref, spread_ref, coupling_ref, diagonal_ref,
    send_ref, own_ref, q_ref, scale_ref, partial_ref,
):
    b = b_ref[...]
    rows, width = b.shape
    top = pairwise(jnp.maximum, tails_of(recv_ref, rows))
    size, reach = top[:, 0:1], top[:, 1:2]
    scale = jnp.where((size > 0) & (reach > 0), size / reach, 1.0)
    q = chunks_of(recv_ref, own_in)
    q_ref[...] = q
    scale_ref[...] = jnp.broadcast_to(scale, (1, width))
    tail = pack([total(b * b), total(b * q)], width)
    z = apply_m(band_ref, scale * q)
    emit(z, tail, spread_ref, coupling_ref, diagonal_ref, partial_ref, own_ref, send_ref)


def scalars_of(recv_ref, rows, count, repeats):
    summed = pairwise(jnp.add, tails_of(recv_ref, rows)) * (1.0 / repeats)
    return [summed[:, n : n + 1] for n in range(count)]


def third_kernel(
    recv_ref, own_in, b_ref, q_ref, scale_ref, band_ref, spread_ref, coupling_ref, diagonal_ref,
    send_ref, own_ref, twice_ref, half_ref, u_ref, keep_ref, partial_ref, *, n_cols,
):
    b, q = b_ref[...], q_ref[...]
    rows, width = b.shape
    rho, cross = scalars_of(recv_ref, rows, 2, n_cols)
    alpha = rho / cross
    u = (alpha / scale_ref[:, 0:1]) * chunks_of(recv_ref, own_in)
    twice = q - u
    half = b - alpha * q
    tail = pack([total(twice * half), total(twice * twice), total(b * half), total(b * twice)], width)
    twice_ref[...], half_ref[...], u_ref[...] = twice, half, u
    keep_ref[...] = pack([rho, alpha], width)
    z = apply_m(band_ref, alpha * twice)
    emit(z, tail, spread_ref, coupling_ref, diagonal_ref, partial_ref, own_ref, send_ref)


def fourth_kernel(
    recv_ref, own_in, b_ref, q_ref, twice_ref, half_ref, u_ref, keep_ref, band_ref, halves_ref, coupling_ref,
    diagonal_ref, *refs, n_rows, n_cols, n_sub,
):
    parts, (three_ref, search_ref, done_ref, kept_ref, partial_ref, own_ref) = refs[:n_sub], refs[n_sub:]
    b, q, twice, half = b_ref[...], q_ref[...], twice_ref[...], half_ref[...]
    rows, width = b.shape
    rho, alpha = keep_ref[:, 0:1], keep_ref[:, 1:2]
    cross, square, b_half, b_twice = scalars_of(recv_ref, rows, 4, n_cols)
    omega = cross / square
    rho_next = b_half - omega * b_twice
    ratio = rho_next / rho
    beta = ratio * (alpha / omega)
    a = twice - (omega / alpha) * chunks_of(recv_ref, own_in)
    residual = half - omega * twice
    image = a + beta * q - ratio * u_ref[...]
    three_ref[...] = jnp.concatenate([a, residual, image], axis=0)
    search_ref[...] = residual + beta * (b - omega * q)
    done_ref[...] = alpha * b + omega * half
    kept_ref[...] = pack([rho_next, alpha], width)
    first = lax.axis_index("cols") == 0
    tail = pack([jnp.where(first, total(b * image), 0.0)], width)
    z = apply_m(band_ref, alpha * image)
    products(z, coupling_ref, diagonal_ref, partial_ref, own_ref)
    out = jnp.dot(halves_ref[...], split3(partial_ref[...]), preferred_element_type=jnp.float32)
    size = parts[0].shape[0]
    for t, part_ref in enumerate(parts):
        part_ref[...] = out[t * size : (t + 1) * size]
        part_ref[pl.ds(n_rows * rows, 1), :] = tail
    here = pl.ds(pl.multiple_of(lax.axis_index("rows") * rows, rows), rows)
    parts[0][here, :] = parts[0][here, :] + jnp.where(first, own_ref[...], 0.0)


def fifth_kernel(mine_ref, *refs, order, n_rows):
    others, (kept_ref, search_ref, done_ref, twice_ref, half_ref, sum_ref, dots_ref, full_ref) = (
        refs[: n_rows - 1],
        refs[n_rows - 1 :],
    )
    rows, width = search_ref.shape
    size = full_ref.shape[0]
    full = mine_ref[pl.ds(0, size), :]
    for other in others:
        full = full + other[pl.ds(0, size), :]
    full_ref[...] = full
    tail = full[n_rows * rows : n_rows * rows + 1]
    alpha = kept_ref[:, 0:1] / tail[:, 0:1]
    factor = alpha / kept_ref[:, 1:2]
    own = lax.axis_index("rows")
    cross = square = None
    for step, source in [(0, mine_ref)] + [(n + 1, other) for n, other in zip(order, others)]:
        at = own if step == 0 else sender(own, step, n_rows)
        a, residual, image = (source[pl.ds(size + n * rows, rows), :] for n in range(3))
        twice = a - factor * full_ref[pl.ds(pl.multiple_of(at * rows, rows), rows), :]
        half = residual - alpha * image
        if step == 0:
            twice_ref[...], half_ref[...] = twice, half
            cross, square = twice * half, twice * twice
        else:
            cross, square = cross + twice * half, square + twice * twice
    sum_ref[...] = done_ref[...] + alpha * search_ref[...]
    dots_ref[...] = pack([total(cross), total(square)], width)


def map_kernel(half_ref, sum_ref, band_ref, half_hat_ref, sum_hat_ref):
    half_hat_ref[...] = apply_m(band_ref, half_ref[...])
    sum_hat_ref[...] = apply_m(band_ref, sum_ref[...])


def last_kernel(twice_ref, half_ref, half_hat_ref, sum_hat_ref, *refs):
    *shares, solution_ref, residual_ref = refs
    dots = functools.reduce(jnp.add, [share[...] for share in shares])
    omega = dots[:, 0:1] / dots[:, 1:2]
    residual_ref[...] = half_ref[...] - omega * twice_ref[...]
    solution_ref[...] = sum_hat_ref[...] + omega * half_hat_ref[...]


def partner(at, step, count):
    return at ^ step if count & (count - 1) == 0 else (at + step) % count


def sender(at, step, count):
    return at ^ step if count & (count - 1) == 0 else (at + count - step) % count


def shifted(x, axis, step):
    count = lax.axis_size(axis)
    return lax.ppermute(x, axis, [(i, partner(i, step, count)) for i in range(count)])


def sum_over(x, axis):
    out = x
    for step in range(1, lax.axis_size(axis)):
        out = out + shifted(x, axis, step)
    return out


def call(kernel, outs, args, scratch=(), space=pltpu.VMEM):
    spec = pl.BlockSpec(memory_space=pltpu.VMEM)
    if space == pltpu.HBM:
        args = [pltpu.with_memory_space_constraint(x, space) for x in args]
    return pl.pallas_call(
        kernel,
        out_shape=[pltpu.VMEM(shape, kind) if space == pltpu.HBM else jax.ShapeDtypeStruct(shape, kind) for shape, kind in outs],
        in_specs=[pl.BlockSpec(memory_space=space)] * len(args),
        out_specs=[spec] * len(outs),
        scratch_shapes=list(scratch),
        compiler_params=pltpu.CompilerParams(vmem_limit_bytes=24 << 20),
    )(*args)


def on_device(diagonal, coupling, column_part, column_tile, neighbours, b, jacobi):
    f32 = jnp.float32
    rows, width = b.shape
    slots = coupling.shape[1]
    sizes = tuple(lax.axis_size(axis) for axis in ("rows", "cols", "sub"))
    n_rows, n_cols, n_sub = sizes
    devices = n_rows * n_cols * n_sub
    vec, line = ((rows, width), f32), ((1, width), f32)
    message = ((devices * (rows + 1), width), f32)
    part_size = n_rows * rows + 8
    part_shape = ((part_size, width), f32)
    band_shape = ((2 * BAND + 1, rows, width), f32)
    spread_shape = ((devices * (rows + 1), 3 * slots * rows), jnp.bfloat16)
    halves_shape = ((n_sub * part_size, 3 * slots * rows), jnp.bfloat16)
    scratch = [pltpu.VMEM((slots * rows, width), f32)]

    def exchange(send):
        send = send.reshape(devices, rows + 1, 1, width)
        return lax.all_to_all(send, PART, 0, 0, tiled=True).reshape(devices * (rows + 1), width)

    part, tile = column_part.T, column_tile.T
    sems = [pltpu.SemaphoreType.DMA((n,)) for n in (4, rows // 8, rows // 8, rows // 8)]
    send, own, band, spread, halves, b, coupling, diagonal = call(
        functools.partial(first_kernel, sizes=sizes),
        [message, vec, band_shape, spread_shape, halves_shape, vec, (coupling.shape, f32), (diagonal.shape, f32)],
        (b, jacobi, part, tile, neighbours, coupling, diagonal),
        scratch
        + [pltpu.VMEM(jacobi.shape, f32)]
        + [pltpu.VMEM(x.shape, x.dtype) for x in (part, tile, neighbours)]
        + sems,
        pltpu.HBM,
    )
    tiles = (coupling, diagonal)
    send, own, q, scale = call(
        second_kernel, [message, vec, vec, line], (exchange(send), own, b, band, spread) + tiles, scratch
    )
    send, own, twice, half, u, keep = call(
        functools.partial(third_kernel, n_cols=n_cols), [message] + [vec] * 4 + [line],
        (exchange(send), own, b, q, scale, band, spread) + tiles, scratch,
    )
    *parts, three, search, done, kept = call(
        functools.partial(fourth_kernel, n_rows=n_rows, n_cols=n_cols, n_sub=n_sub),
        [part_shape] * n_sub + [((3 * rows, width), f32), vec, vec, line],
        (exchange(send), own, b, q, twice, half, u, keep, band, halves) + tiles,
        scratch + [pltpu.VMEM((rows, width), f32)],
    )
    summed = parts[0]
    for step in range(1, n_sub):
        summed = summed + shifted(parts[step], "sub", step)
    summed = sum_over(summed, "cols")
    mine = jnp.concatenate([summed, three])
    others = [shifted(mine, "rows", step) for step in range(1, n_rows)]
    order = [1, 0, *range(2, n_rows - 1)]
    twice, half, total_search, dots = call(
        functools.partial(fifth_kernel, order=order, n_rows=n_rows), [vec] * 3 + [line],
        (mine, *(others[n] for n in order), kept, search, done), [pltpu.VMEM((part_size, width), f32)],
    )
    half_hat, sum_hat = call(map_kernel, [vec, vec], (half, total_search, band))
    shares = [dots] + [shifted(dots, "sub", step) for step in range(1, n_sub)]
    return tuple(call(last_kernel, [vec, vec], (twice, half, half_hat, sum_hat, *shares)))


def solution(mesh):
    lines = P(("groups", "rows", "sub"), None)
    tiles = P(("groups", "rows", "sub"), None, None)
    slots = P(("groups", "rows", "sub"), "cols")
    in_specs = (
        tiles, P(("groups", "rows", "sub"), "cols", None, None), slots, slots, P("groups", None), lines, tiles,
    )
    return jax.shard_map(on_device, mesh=mesh, in_specs=in_specs, out_specs=(lines, lines), check_vma=False)
```

```python
import functools

import jax
import jax.numpy as jnp
from jax import lax
from jax.experimental import pallas as pl
from jax.experimental.pallas import tpu as pltpu
from jax.sharding import PartitionSpec as P

BLOCK = 5
BAND = BLOCK - 1
LANES = 128
PART = ("rows", "sub", "cols")


def apply_m(band_ref, v):
    width = v.shape[1]
    z = band_ref[BAND] * v
    for d in range(-BAND, BAND + 1):
        if d:
            z = z + band_ref[d + BAND] * pltpu.roll(v, (-d) % width, 1)
    return z


def split3(x):
    hi = x.astype(jnp.bfloat16)
    rest = x - hi.astype(jnp.float32)
    mid = rest.astype(jnp.bfloat16)
    low = (rest - mid.astype(jnp.float32)).astype(jnp.bfloat16)
    return jnp.concatenate([hi, mid, low], axis=0)


def sum_lines(parts):
    line = lax.broadcasted_iota(jnp.int32, parts[0].shape, 0)
    step = 1
    while len(parts) > 1:
        low = (line // step) % 2 == 0
        parts = [
            jnp.where(low, one, two) + pltpu.roll(jnp.where(low, two, one), step, 0)
            for one, two in zip(parts[::2], parts[1::2])
        ]
        step *= 2
    return parts[0]


def folded(column, tile):
    width = tile.shape[1]
    return jnp.sum((column * tile).reshape(width // 8, 8, width), axis=0)


def spread_products(z, spread_ref, coupling_ref, diagonal_ref, scratch, own_ref, before=None):
    partial_ref, column_ref = scratch
    rows, slots, width = coupling_ref.shape[:3]
    for first in range(0, rows, 8):
        if before is not None:
            before(first // 8)
        sums = [[] for _ in range(slots)]
        for r in range(first, first + 8):
            column = jnp.broadcast_to(z[r : r + 1], (width, width)).T
            column_ref[r] = column
            for k in range(slots):
                sums[k].append(folded(column, coupling_ref[r, k]))
        for k in range(slots):
            partial_ref[pl.ds(k * rows + first, 8), :] = sum_lines(sums[k])
    if before is not None:
        before(rows // 8)
    out = jnp.dot(spread_ref[...], split3(partial_ref[...]), preferred_element_type=jnp.float32)
    for first in range(0, rows, 8):
        own_ref[pl.ds(first, 8), :] = sum_lines([folded(column_ref[r], diagonal_ref[r]) for r in range(first, first + 8)])
    return out


def emit(z, tail, spread_ref, coupling_ref, diagonal_ref, scratch, own_ref, send_ref, before=None):
    rows = z.shape[0]
    send_ref[...] = spread_products(z, spread_ref, coupling_ref, diagonal_ref, scratch, own_ref, before)
    if callable(tail):
        tail = tail()
    for d in range(send_ref.shape[0] // (rows + 1)):
        send_ref[pl.ds(d * (rows + 1) + rows, 1), :] = tail


def pack(scalars, width):
    lane = lax.broadcasted_iota(jnp.int32, (1, width), 1)
    tail = jnp.zeros((1, width), jnp.float32)
    for at, value in enumerate(scalars):
        tail = jnp.where(lane == at, value, tail)
    return tail


def total(x):
    return jnp.sum(jnp.sum(x, axis=0, keepdims=True), axis=1, keepdims=True)


def peak(x):
    return jnp.max(jnp.max(jnp.abs(x), axis=0, keepdims=True), axis=1, keepdims=True)


def pairwise(join, items):
    items = list(items)
    while len(items) > 1:
        items = [join(*items[n : n + 2]) if n + 1 < len(items) else items[n] for n in range(0, len(items), 2)]
    return items[0]


def tails_of(recv_ref, rows):
    count = recv_ref.shape[0] // (rows + 1)
    return [recv_ref[pl.ds(d * (rows + 1) + rows, 1), :] for d in range(count)]


def chunk(recv_ref, d, rows):
    return recv_ref[pl.ds(d * (rows + 1), rows), :]


def chunks_of(recv_ref, own_in):
    rows = own_in.shape[0]
    return pairwise(jnp.add, [own_in[...]] + [chunk(recv_ref, d, rows) for d in range(recv_ref.shape[0] // (rows + 1))])


def first_kernel(
    b_hbm, jacobi_hbm, part_hbm, tile_hbm, near_hbm, coupling_hbm, diagonal_hbm,
    send_ref, own_ref, band_ref, spread_ref, halves_ref, b_ref, coupling_ref, diagonal_ref,
    partial_ref, column_ref, jacobi_ref, part_ref, tile_ref, near_ref, small_sem, jacobi_sem, coupling_sem, diagonal_sem,
    *, sizes,
):
    n_rows, n_cols, n_sub = sizes
    rows, slots = coupling_ref.shape[0], coupling_ref.shape[1]
    width = b_ref.shape[1]
    groups = rows // 8

    def some(ref, g):
        return ref.at[pl.ds(g * 8, 8)]

    def copy_of(g, source, target, sem):
        return pltpu.make_async_copy(some(source, g), some(target, g), sem.at[g])

    small = [
        pltpu.make_async_copy(source, target, small_sem.at[n])
        for n, (source, target) in enumerate(
            ((b_hbm, b_ref), (part_hbm, part_ref), (tile_hbm, tile_ref), (near_hbm, near_ref))
        )
    ]
    for copy in small:
        copy.start()
    for g in range(groups):
        copy_of(g, jacobi_hbm, jacobi_ref, jacobi_sem).start()
    for g in range(groups):
        copy_of(g, coupling_hbm, coupling_ref, coupling_sem).start()
    diagonal_copy = pltpu.make_async_copy(diagonal_hbm, diagonal_ref, diagonal_sem)
    diagonal_copy.start()
    for copy in small:
        copy.wait()
    own = lax.axis_index("rows")
    part, tile, near = part_ref[...], tile_ref[...], near_ref[...]
    near_row = lax.broadcasted_iota(jnp.int32, near.shape, 0)
    mine = jnp.sum(jnp.where(near_row == own, near, 0), axis=0, keepdims=True)
    target = jnp.where(part == 0, own, 0)
    for n in range(near.shape[1]):
        target = target + jnp.where(part == n + 1, mine[:, n : n + 1], 0)
    landing = target * (rows * n_sub) + tile
    landing = jnp.concatenate([landing[k : k + 1] for k in range(slots)] * 3, axis=1)
    at = lax.broadcasted_iota(jnp.int32, (spread_ref.shape[0], 1), 0)
    device, line = at // (rows + 1), at % (rows + 1)
    row, sub = device // (n_cols * n_sub), device // n_cols % n_sub
    wanted = jnp.where(line < rows, row * (rows * n_sub) + sub * rows + line, -1)
    spread_ref[...] = jnp.where(landing == wanted, 1.0, 0.0).astype(jnp.bfloat16)
    at = lax.broadcasted_iota(jnp.int32, (halves_ref.shape[0], 1), 0)
    size = halves_ref.shape[0] // n_sub
    sub, at = partner(lax.axis_index("sub"), at // size, n_sub), at % size
    wanted = jnp.where(at < n_rows * rows, at // rows * (rows * n_sub) + sub * rows + at % rows, -1)
    halves_ref[...] = jnp.where(landing == wanted, 1.0, 0.0).astype(jnp.bfloat16)
    m = lax.broadcasted_iota(jnp.int32, (1, 8, width), 1)
    j = lax.broadcasted_iota(jnp.int32, (1, 8, width), 2)
    last = width // BLOCK * BLOCK
    for g in range(groups):
        copy_of(g, jacobi_hbm, jacobi_ref, jacobi_sem).wait()
        folded = jnp.sum(some(jacobi_ref, g)[...].reshape(8, width // 8, 8, width), axis=1)
        for d in range(-BAND, BAND + 1):
            i = j + d
            inside = (i // BLOCK == j // BLOCK) & (j < last) if d else j >= 0
            picked = inside & (i >= 0) & (lax.rem(i + 8, 8) == m)
            band_ref[d + BAND, pl.ds(g * 8, 8)] = jnp.sum(jnp.where(picked, folded, 0.0), axis=1)
    z = apply_m(band_ref, b_ref[...])

    def before(g):
        (copy_of(g, coupling_hbm, coupling_ref, coupling_sem) if g < groups else diagonal_copy).wait()

    def tail():
        return pack([peak(b_ref[...]), jnp.maximum(peak(partial_ref[...]), peak(own_ref[...]))], width)

    emit(z, tail, spread_ref, coupling_ref, diagonal_ref, (partial_ref, column_ref), own_ref, send_ref, before)


def second_kernel(
    recv_ref, own_in, b_ref, band_ref, spread_ref, coupling_ref, diagonal_ref,
    send_ref, own_ref, q_ref, scale_ref, partial_ref, column_ref,
):
    b = b_ref[...]
    rows, width = b.shape
    top = pairwise(jnp.maximum, tails_of(recv_ref, rows))
    size, reach = top[:, 0:1], top[:, 1:2]
    scale = jnp.where((size > 0) & (reach > 0), size / reach, 1.0)
    q = chunks_of(recv_ref, own_in)
    q_ref[...] = q
    scale_ref[...] = jnp.broadcast_to(scale, (1, width))
    tail = pack([total(b * b), total(b * q)], width)
    z = apply_m(band_ref, scale * q)
    emit(z, tail, spread_ref, coupling_ref, diagonal_ref, (partial_ref, column_ref), own_ref, send_ref)


def scalars_of(recv_ref, rows, count, repeats):
    summed = pairwise(jnp.add, tails_of(recv_ref, rows)) * (1.0 / repeats)
    return [summed[:, n : n + 1] for n in range(count)]


def third_kernel(
    recv_ref, own_in, b_ref, q_ref, scale_ref, band_ref, spread_ref, coupling_ref, diagonal_ref,
    send_ref, own_ref, twice_ref, half_ref, u_ref, keep_ref, partial_ref, column_ref, *, n_cols,
):
    b, q = b_ref[...], q_ref[...]
    rows, width = b.shape
    rho, cross = scalars_of(recv_ref, rows, 2, n_cols)
    alpha = rho / cross
    u = (alpha / scale_ref[:, 0:1]) * chunks_of(recv_ref, own_in)
    twice = q - u
    half = b - alpha * q
    tail = pack([total(twice * half), total(twice * twice), total(b * half), total(b * twice)], width)
    twice_ref[...], half_ref[...], u_ref[...] = twice, half, u
    keep_ref[...] = pack([rho, alpha], width)
    z = apply_m(band_ref, alpha * twice)
    emit(z, tail, spread_ref, coupling_ref, diagonal_ref, (partial_ref, column_ref), own_ref, send_ref)


def fourth_kernel(
    recv_ref, own_in, b_ref, q_ref, twice_ref, half_ref, u_ref, keep_ref, band_ref, halves_ref, coupling_ref,
    diagonal_ref, *refs, n_rows, n_cols, n_sub,
):
    parts, (three_ref, search_ref, done_ref, kept_ref, partial_ref, column_ref, own_ref) = refs[:n_sub], refs[n_sub:]
    b, q, twice, half = b_ref[...], q_ref[...], twice_ref[...], half_ref[...]
    rows, width = b.shape
    rho, alpha = keep_ref[:, 0:1], keep_ref[:, 1:2]
    cross, square, b_half, b_twice = scalars_of(recv_ref, rows, 4, n_cols)
    omega = cross / square
    rho_next = b_half - omega * b_twice
    ratio = rho_next / rho
    beta = ratio * (alpha / omega)
    a = twice - (omega / alpha) * chunks_of(recv_ref, own_in)
    residual = half - omega * twice
    image = a + beta * q - ratio * u_ref[...]
    three_ref[...] = jnp.concatenate([a, residual, image], axis=0)
    search_ref[...] = residual + beta * (b - omega * q)
    done_ref[...] = alpha * b + omega * half
    kept_ref[...] = pack([rho_next, alpha], width)
    first = lax.axis_index("cols") == 0
    tail = pack([jnp.where(first, total(b * image), 0.0)], width)
    z = apply_m(band_ref, alpha * image)
    out = spread_products(z, halves_ref, coupling_ref, diagonal_ref, (partial_ref, column_ref), own_ref)
    size = parts[0].shape[0]
    for t, part_ref in enumerate(parts):
        part_ref[...] = out[t * size : (t + 1) * size]
        part_ref[pl.ds(n_rows * rows, 1), :] = tail
    here = pl.ds(pl.multiple_of(lax.axis_index("rows") * rows, rows), rows)
    parts[0][here, :] = parts[0][here, :] + jnp.where(first, own_ref[...], 0.0)


def fifth_kernel(mine_ref, *refs, order, n_rows):
    others, (kept_ref, search_ref, done_ref, twice_ref, half_ref, sum_ref, dots_ref, full_ref) = (
        refs[: n_rows - 1],
        refs[n_rows - 1 :],
    )
    rows, width = search_ref.shape
    size = full_ref.shape[0]
    full = mine_ref[pl.ds(0, size), :]
    for other in others:
        full = full + other[pl.ds(0, size), :]
    full_ref[...] = full
    tail = full[n_rows * rows : n_rows * rows + 1]
    alpha = kept_ref[:, 0:1] / tail[:, 0:1]
    factor = alpha / kept_ref[:, 1:2]
    own = lax.axis_index("rows")
    cross = square = None
    for step, source in [(0, mine_ref)] + [(n + 1, other) for n, other in zip(order, others)]:
        at = own if step == 0 else sender(own, step, n_rows)
        a, residual, image = (source[pl.ds(size + n * rows, rows), :] for n in range(3))
        twice = a - factor * full_ref[pl.ds(pl.multiple_of(at * rows, rows), rows), :]
        half = residual - alpha * image
        if step == 0:
            twice_ref[...], half_ref[...] = twice, half
            cross, square = twice * half, twice * twice
        else:
            cross, square = cross + twice * half, square + twice * twice
    sum_ref[...] = done_ref[...] + alpha * search_ref[...]
    dots_ref[...] = pack([total(cross), total(square)], width)


def map_kernel(half_ref, sum_ref, band_ref, half_hat_ref, sum_hat_ref):
    half_hat_ref[...] = apply_m(band_ref, half_ref[...])
    sum_hat_ref[...] = apply_m(band_ref, sum_ref[...])


def last_kernel(twice_ref, half_ref, half_hat_ref, sum_hat_ref, *refs):
    *shares, solution_ref, residual_ref = refs
    dots = functools.reduce(jnp.add, [share[...] for share in shares])
    omega = dots[:, 0:1] / dots[:, 1:2]
    residual_ref[...] = half_ref[...] - omega * twice_ref[...]
    solution_ref[...] = sum_hat_ref[...] + omega * half_hat_ref[...]


def partner(at, step, count):
    return at ^ step if count & (count - 1) == 0 else (at + step) % count


def sender(at, step, count):
    return at ^ step if count & (count - 1) == 0 else (at + count - step) % count


def shifted(x, axis, step):
    count = lax.axis_size(axis)
    return lax.ppermute(x, axis, [(i, partner(i, step, count)) for i in range(count)])


def sum_over(x, axis):
    out = x
    for step in range(1, lax.axis_size(axis)):
        out = out + shifted(x, axis, step)
    return out


def call(kernel, outs, args, scratch=(), space=pltpu.VMEM):
    spec = pl.BlockSpec(memory_space=pltpu.VMEM)
    if space == pltpu.HBM:
        args = [pltpu.with_memory_space_constraint(x, space) for x in args]
    return pl.pallas_call(
        kernel,
        out_shape=[pltpu.VMEM(shape, kind) if space == pltpu.HBM else jax.ShapeDtypeStruct(shape, kind) for shape, kind in outs],
        in_specs=[pl.BlockSpec(memory_space=space)] * len(args),
        out_specs=[spec] * len(outs),
        scratch_shapes=list(scratch),
        compiler_params=pltpu.CompilerParams(vmem_limit_bytes=24 << 20),
    )(*args)


def on_device(diagonal, coupling, column_part, column_tile, neighbours, b, jacobi):
    f32 = jnp.float32
    rows, width = b.shape
    slots = coupling.shape[1]
    sizes = tuple(lax.axis_size(axis) for axis in ("rows", "cols", "sub"))
    n_rows, n_cols, n_sub = sizes
    devices = n_rows * n_cols * n_sub
    vec, line = ((rows, width), f32), ((1, width), f32)
    message = ((devices * (rows + 1), width), f32)
    part_size = n_rows * rows + 8
    part_shape = ((part_size, width), f32)
    band_shape = ((2 * BAND + 1, rows, width), f32)
    spread_shape = ((devices * (rows + 1), 3 * slots * rows), jnp.bfloat16)
    halves_shape = ((n_sub * part_size, 3 * slots * rows), jnp.bfloat16)
    scratch = [pltpu.VMEM((slots * rows, width), f32), pltpu.VMEM((rows, width, width), f32)]

    def exchange(send):
        send = send.reshape(devices, rows + 1, 1, width)
        return lax.all_to_all(send, PART, 0, 0, tiled=True).reshape(devices * (rows + 1), width)

    part, tile = column_part.T, column_tile.T
    sems = [pltpu.SemaphoreType.DMA((n,)) for n in (4, rows // 8, rows // 8)] + [pltpu.SemaphoreType.DMA]
    send, own, band, spread, halves, b, coupling, diagonal = call(
        functools.partial(first_kernel, sizes=sizes),
        [message, vec, band_shape, spread_shape, halves_shape, vec, (coupling.shape, f32), (diagonal.shape, f32)],
        (b, jacobi, part, tile, neighbours, coupling, diagonal),
        scratch
        + [pltpu.VMEM(jacobi.shape, f32)]
        + [pltpu.VMEM(x.shape, x.dtype) for x in (part, tile, neighbours)]
        + sems,
        pltpu.HBM,
    )
    tiles = (coupling, diagonal)
    send, own, q, scale = call(
        second_kernel, [message, vec, vec, line], (exchange(send), own, b, band, spread) + tiles, scratch
    )
    send, own, twice, half, u, keep = call(
        functools.partial(third_kernel, n_cols=n_cols), [message] + [vec] * 4 + [line],
        (exchange(send), own, b, q, scale, band, spread) + tiles, scratch,
    )
    *parts, three, search, done, kept = call(
        functools.partial(fourth_kernel, n_rows=n_rows, n_cols=n_cols, n_sub=n_sub),
        [part_shape] * n_sub + [((3 * rows, width), f32), vec, vec, line],
        (exchange(send), own, b, q, twice, half, u, keep, band, halves) + tiles,
        scratch + [pltpu.VMEM((rows, width), f32)],
    )
    summed = parts[0]
    for step in range(1, n_sub):
        summed = summed + shifted(parts[step], "sub", step)
    summed = sum_over(summed, "cols")
    mine = jnp.concatenate([summed, three])
    others = [shifted(mine, "rows", step) for step in range(1, n_rows)]
    order = [1, 0, *range(2, n_rows - 1)]
    twice, half, total_search, dots = call(
        functools.partial(fifth_kernel, order=order, n_rows=n_rows), [vec] * 3 + [line],
        (mine, *(others[n] for n in order), kept, search, done), [pltpu.VMEM((part_size, width), f32)],
    )
    half_hat, sum_hat = call(map_kernel, [vec, vec], (half, total_search, band))
    shares = [dots] + [shifted(dots, "sub", step) for step in range(1, n_sub)]
    return tuple(call(last_kernel, [vec, vec], (twice, half, half_hat, sum_hat, *shares)))


def solution(mesh):
    lines = P(("groups", "rows", "sub"), None)
    tiles = P(("groups", "rows", "sub"), None, None)
    slots = P(("groups", "rows", "sub"), "cols")
    in_specs = (
        tiles, P(("groups", "rows", "sub"), "cols", None, None), slots, slots, P("groups", None), lines, tiles,
    )
    return jax.shard_map(on_device, mesh=mesh, in_specs=in_specs, out_specs=(lines, lines), check_vma=False)
```

```python
import functools

import jax
import jax.numpy as jnp
from jax import lax
from jax.experimental import pallas as pl
from jax.experimental.pallas import tpu as pltpu
from jax.sharding import PartitionSpec as P

BLOCK = 5
BAND = BLOCK - 1
LANES = 128
PART = ("rows", "sub", "cols")


def apply_m(band_ref, v):
    width = v.shape[1]
    z = band_ref[BAND] * v
    for d in range(-BAND, BAND + 1):
        if d:
            z = z + band_ref[d + BAND] * pltpu.roll(v, (-d) % width, 1)
    return z


def split3(x):
    hi = x.astype(jnp.bfloat16)
    rest = x - hi.astype(jnp.float32)
    mid = rest.astype(jnp.bfloat16)
    low = (rest - mid.astype(jnp.float32)).astype(jnp.bfloat16)
    return jnp.concatenate([hi, mid, low], axis=0)


def sum_lines(parts):
    line = lax.broadcasted_iota(jnp.int32, parts[0].shape, 0)
    step = 1
    while len(parts) > 1:
        low = (line // step) % 2 == 0
        parts = [
            jnp.where(low, one, two) + pltpu.roll(jnp.where(low, two, one), step, 0)
            for one, two in zip(parts[::2], parts[1::2])
        ]
        step *= 2
    return parts[0]


def folded(column, tile):
    width = tile.shape[1]
    return jnp.sum((column * tile).reshape(width // 8, 8, width), axis=0)


def spread_products(z, spread_ref, coupling_ref, diagonal_ref, scratch, own_ref, before=None):
    partial_ref, column_ref = scratch
    rows, slots, width = coupling_ref.shape[:3]
    for first in range(0, rows, 8):
        if before is not None:
            before(first // 8)
        sums = [[] for _ in range(slots)]
        for r in range(first, first + 8):
            column = jnp.broadcast_to(z[r : r + 1], (width, width)).T
            column_ref[r] = column
            for k in range(slots):
                sums[k].append(folded(column, coupling_ref[r, k]))
        for k in range(slots):
            partial_ref[pl.ds(k * rows + first, 8), :] = sum_lines(sums[k])
    if before is not None:
        before(rows // 8)
    out = jnp.dot(spread_ref[...], split3(partial_ref[...]), preferred_element_type=jnp.float32)
    for first in range(0, rows, 8):
        own_ref[pl.ds(first, 8), :] = sum_lines([folded(column_ref[r], diagonal_ref[r]) for r in range(first, first + 8)])
    return out


def emit(z, tail, spread_ref, coupling_ref, diagonal_ref, scratch, own_ref, send_ref, before=None):
    rows = z.shape[0]
    send_ref[...] = spread_products(z, spread_ref, coupling_ref, diagonal_ref, scratch, own_ref, before)
    if callable(tail):
        tail = tail()
    for d in range(send_ref.shape[0] // (rows + 1)):
        send_ref[pl.ds(d * (rows + 1) + rows, 1), :] = tail


def pack(scalars, width):
    lane = lax.broadcasted_iota(jnp.int32, (1, width), 1)
    tail = jnp.zeros((1, width), jnp.float32)
    for at, value in enumerate(scalars):
        tail = jnp.where(lane == at, value, tail)
    return tail


def total(x):
    return jnp.sum(jnp.sum(x, axis=0, keepdims=True), axis=1, keepdims=True)


def peak(x):
    return jnp.max(jnp.max(jnp.abs(x), axis=0, keepdims=True), axis=1, keepdims=True)


def pairwise(join, items):
    items = list(items)
    while len(items) > 1:
        items = [join(*items[n : n + 2]) if n + 1 < len(items) else items[n] for n in range(0, len(items), 2)]
    return items[0]


def tails_of(recv_ref, rows):
    count = recv_ref.shape[0] // (rows + 1)
    return [recv_ref[pl.ds(d * (rows + 1) + rows, 1), :] for d in range(count)]


def chunk(recv_ref, d, rows):
    return recv_ref[pl.ds(d * (rows + 1), rows), :]


def chunks_of(recv_ref, own_in):
    rows = own_in.shape[0]
    return pairwise(jnp.add, [own_in[...]] + [chunk(recv_ref, d, rows) for d in range(recv_ref.shape[0] // (rows + 1))])


def first_kernel(
    b_hbm, jacobi_hbm, part_hbm, tile_hbm, near_hbm, coupling_hbm, diagonal_hbm,
    send_ref, own_ref, band_ref, spread_ref, halves_ref, b_ref, coupling_ref, diagonal_ref,
    partial_ref, column_ref, jacobi_ref, part_ref, tile_ref, near_ref, small_sem, jacobi_sem, coupling_sem, diagonal_sem,
    *, sizes,
):
    n_rows, n_cols, n_sub = sizes
    rows, slots = coupling_ref.shape[0], coupling_ref.shape[1]
    width = b_ref.shape[1]
    groups = rows // 8

    def some(ref, g):
        return ref.at[pl.ds(g * 8, 8)]

    def copy_of(g, source, target, sem):
        return pltpu.make_async_copy(some(source, g), some(target, g), sem.at[g])

    small = [
        pltpu.make_async_copy(source, target, small_sem.at[n])
        for n, (source, target) in enumerate(
            ((b_hbm, b_ref), (part_hbm, part_ref), (tile_hbm, tile_ref), (near_hbm, near_ref))
        )
    ]
    for copy in small:
        copy.start()
    for g in range(groups):
        copy_of(g, jacobi_hbm, jacobi_ref, jacobi_sem).start()
    for g in range(groups):
        copy_of(g, coupling_hbm, coupling_ref, coupling_sem).start()
    diagonal_copy = pltpu.make_async_copy(diagonal_hbm, diagonal_ref, diagonal_sem)
    diagonal_copy.start()
    for copy in small:
        copy.wait()
    own = lax.axis_index("rows")
    part, tile, near = part_ref[...], tile_ref[...], near_ref[...]
    near_row = lax.broadcasted_iota(jnp.int32, near.shape, 0)
    mine = jnp.sum(jnp.where(near_row == own, near, 0), axis=0, keepdims=True)
    target = jnp.where(part == 0, own, 0)
    for n in range(near.shape[1]):
        target = target + jnp.where(part == n + 1, mine[:, n : n + 1], 0)
    landing = target * (rows * n_sub) + tile
    landing = jnp.concatenate([landing[k : k + 1] for k in range(slots)] * 3, axis=1)
    at = lax.broadcasted_iota(jnp.int32, (spread_ref.shape[0], 1), 0)
    device, line = at // (rows + 1), at % (rows + 1)
    row, sub = device // (n_cols * n_sub), device // n_cols % n_sub
    wanted = jnp.where(line < rows, row * (rows * n_sub) + sub * rows + line, -1)
    spread_ref[...] = jnp.where(landing == wanted, 1.0, 0.0).astype(jnp.bfloat16)
    at = lax.broadcasted_iota(jnp.int32, (halves_ref.shape[0], 1), 0)
    size = halves_ref.shape[0] // n_sub
    sub, at = partner(lax.axis_index("sub"), at // size, n_sub), at % size
    wanted = jnp.where(at < n_rows * rows, at // rows * (rows * n_sub) + sub * rows + at % rows, -1)
    halves_ref[...] = jnp.where(landing == wanted, 1.0, 0.0).astype(jnp.bfloat16)
    m = lax.broadcasted_iota(jnp.int32, (1, 8, width), 1)
    j = lax.broadcasted_iota(jnp.int32, (1, 8, width), 2)
    last = width // BLOCK * BLOCK
    for g in range(groups):
        copy_of(g, jacobi_hbm, jacobi_ref, jacobi_sem).wait()
        folded = jnp.sum(some(jacobi_ref, g)[...].reshape(8, width // 8, 8, width), axis=1)
        for d in range(-BAND, BAND + 1):
            i = j + d
            inside = (i // BLOCK == j // BLOCK) & (j < last) if d else j >= 0
            picked = inside & (i >= 0) & (lax.rem(i + 8, 8) == m)
            band_ref[d + BAND, pl.ds(g * 8, 8)] = jnp.sum(jnp.where(picked, folded, 0.0), axis=1)
    z = apply_m(band_ref, b_ref[...])

    def before(g):
        (copy_of(g, coupling_hbm, coupling_ref, coupling_sem) if g < groups else diagonal_copy).wait()

    def tail():
        return pack([peak(b_ref[...]), jnp.maximum(peak(partial_ref[...]), peak(own_ref[...]))], width)

    emit(z, tail, spread_ref, coupling_ref, diagonal_ref, (partial_ref, column_ref), own_ref, send_ref, before)


def second_kernel(
    recv_ref, own_in, b_ref, band_ref, spread_ref, coupling_ref, diagonal_ref,
    send_ref, own_ref, q_ref, scale_ref, partial_ref, column_ref,
):
    b = b_ref[...]
    rows, width = b.shape
    top = pairwise(jnp.maximum, tails_of(recv_ref, rows))
    size, reach = top[:, 0:1], top[:, 1:2]
    scale = jnp.where((size > 0) & (reach > 0), size / reach, 1.0)
    q = chunks_of(recv_ref, own_in)
    q_ref[...] = q
    scale_ref[...] = jnp.broadcast_to(scale, (1, width))
    tail = pack([total(b * b), total(b * q)], width)
    z = apply_m(band_ref, scale * q)
    emit(z, tail, spread_ref, coupling_ref, diagonal_ref, (partial_ref, column_ref), own_ref, send_ref)


def scalars_of(recv_ref, rows, count, repeats):
    summed = pairwise(jnp.add, tails_of(recv_ref, rows)) * (1.0 / repeats)
    return [summed[:, n : n + 1] for n in range(count)]


def third_kernel(
    recv_ref, own_in, b_ref, q_ref, scale_ref, band_ref, spread_ref, coupling_ref, diagonal_ref,
    send_ref, own_ref, twice_ref, half_ref, u_ref, keep_ref, partial_ref, column_ref, *, n_cols,
):
    b, q = b_ref[...], q_ref[...]
    rows, width = b.shape
    rho, cross = scalars_of(recv_ref, rows, 2, n_cols)
    alpha = rho / cross
    u = (alpha / scale_ref[:, 0:1]) * chunks_of(recv_ref, own_in)
    twice = q - u
    half = b - alpha * q
    tail = pack([total(twice * half), total(twice * twice), total(b * half), total(b * twice)], width)
    twice_ref[...], half_ref[...], u_ref[...] = twice, half, u
    scale = scale_ref[:, 0:1]
    keep_ref[...] = pack([rho, alpha, scale], width)
    z = apply_m(band_ref, scale * twice)
    emit(z, tail, spread_ref, coupling_ref, diagonal_ref, (partial_ref, column_ref), own_ref, send_ref)


def fourth_kernel(
    recv_ref, own_in, b_ref, q_ref, twice_ref, half_ref, u_ref, keep_ref, band_ref, halves_ref, coupling_ref,
    diagonal_ref, *refs, n_rows, n_cols, n_sub,
):
    parts, (three_ref, search_ref, done_ref, kept_ref, partial_ref, column_ref, own_ref) = refs[:n_sub], refs[n_sub:]
    b, q, twice, half = b_ref[...], q_ref[...], twice_ref[...], half_ref[...]
    rows, width = b.shape
    rho, alpha, scale = (keep_ref[:, n : n + 1] for n in range(3))
    cross, square, b_half, b_twice = scalars_of(recv_ref, rows, 4, n_cols)
    omega = cross / square
    rho_next = b_half - omega * b_twice
    ratio = rho_next / rho
    beta = ratio * (alpha / omega)
    a = twice - (omega / scale) * chunks_of(recv_ref, own_in)
    residual = half - omega * twice
    image = a + beta * q - ratio * u_ref[...]
    three_ref[...] = jnp.concatenate([a, residual, image], axis=0)
    search_ref[...] = residual + beta * (b - omega * q)
    done_ref[...] = alpha * b + omega * half
    kept_ref[...] = pack([rho_next, scale], width)
    first = lax.axis_index("cols") == 0
    tail = pack([jnp.where(first, total(b * image), 0.0)], width)
    z = apply_m(band_ref, scale * image)
    out = spread_products(z, halves_ref, coupling_ref, diagonal_ref, (partial_ref, column_ref), own_ref)
    size = parts[0].shape[0]
    for t, part_ref in enumerate(parts):
        part_ref[...] = out[t * size : (t + 1) * size]
        part_ref[pl.ds(n_rows * rows, 1), :] = tail
    here = pl.ds(pl.multiple_of(lax.axis_index("rows") * rows, rows), rows)
    parts[0][here, :] = parts[0][here, :] + jnp.where(first, own_ref[...], 0.0)


def fifth_kernel(mine_ref, *refs, order, n_rows):
    others, (kept_ref, search_ref, done_ref, twice_ref, half_ref, sum_ref, dots_ref, full_ref) = (
        refs[: n_rows - 1],
        refs[n_rows - 1 :],
    )
    rows, width = search_ref.shape
    size = full_ref.shape[0]
    full = mine_ref[pl.ds(0, size), :]
    for other in others:
        full = full + other[pl.ds(0, size), :]
    full_ref[...] = full
    tail = full[n_rows * rows : n_rows * rows + 1]
    alpha = kept_ref[:, 0:1] / tail[:, 0:1]
    factor = alpha / kept_ref[:, 1:2]
    own = lax.axis_index("rows")
    cross = square = None
    for step, source in [(0, mine_ref)] + [(n + 1, other) for n, other in zip(order, others)]:
        at = own if step == 0 else sender(own, step, n_rows)
        a, residual, image = (source[pl.ds(size + n * rows, rows), :] for n in range(3))
        twice = a - factor * full_ref[pl.ds(pl.multiple_of(at * rows, rows), rows), :]
        half = residual - alpha * image
        if step == 0:
            twice_ref[...], half_ref[...] = twice, half
            cross, square = twice * half, twice * twice
        else:
            cross, square = cross + twice * half, square + twice * twice
    sum_ref[...] = done_ref[...] + alpha * search_ref[...]
    dots_ref[...] = pack([total(cross), total(square)], width)


def map_kernel(half_ref, sum_ref, band_ref, half_hat_ref, sum_hat_ref):
    half_hat_ref[...] = apply_m(band_ref, half_ref[...])
    sum_hat_ref[...] = apply_m(band_ref, sum_ref[...])


def last_kernel(twice_ref, half_ref, half_hat_ref, sum_hat_ref, *refs):
    *shares, solution_ref, residual_ref = refs
    dots = functools.reduce(jnp.add, [share[...] for share in shares])
    omega = dots[:, 0:1] / dots[:, 1:2]
    residual_ref[...] = half_ref[...] - omega * twice_ref[...]
    solution_ref[...] = sum_hat_ref[...] + omega * half_hat_ref[...]


def partner(at, step, count):
    return at ^ step if count & (count - 1) == 0 else (at + step) % count


def sender(at, step, count):
    return at ^ step if count & (count - 1) == 0 else (at + count - step) % count


def shifted(x, axis, step):
    count = lax.axis_size(axis)
    return lax.ppermute(x, axis, [(i, partner(i, step, count)) for i in range(count)])


def sum_over(x, axis):
    out = x
    for step in range(1, lax.axis_size(axis)):
        out = out + shifted(x, axis, step)
    return out


def call(kernel, outs, args, scratch=(), space=pltpu.VMEM):
    spec = pl.BlockSpec(memory_space=pltpu.VMEM)
    if space == pltpu.HBM:
        args = [pltpu.with_memory_space_constraint(x, space) for x in args]
    return pl.pallas_call(
        kernel,
        out_shape=[pltpu.VMEM(shape, kind) if space == pltpu.HBM else jax.ShapeDtypeStruct(shape, kind) for shape, kind in outs],
        in_specs=[pl.BlockSpec(memory_space=space)] * len(args),
        out_specs=[spec] * len(outs),
        scratch_shapes=list(scratch),
        compiler_params=pltpu.CompilerParams(vmem_limit_bytes=24 << 20),
    )(*args)


def on_device(diagonal, coupling, column_part, column_tile, neighbours, b, jacobi):
    f32 = jnp.float32
    rows, width = b.shape
    slots = coupling.shape[1]
    sizes = tuple(lax.axis_size(axis) for axis in ("rows", "cols", "sub"))
    n_rows, n_cols, n_sub = sizes
    devices = n_rows * n_cols * n_sub
    vec, line = ((rows, width), f32), ((1, width), f32)
    message = ((devices * (rows + 1), width), f32)
    part_size = n_rows * rows + 8
    part_shape = ((part_size, width), f32)
    band_shape = ((2 * BAND + 1, rows, width), f32)
    spread_shape = ((devices * (rows + 1), 3 * slots * rows), jnp.bfloat16)
    halves_shape = ((n_sub * part_size, 3 * slots * rows), jnp.bfloat16)
    scratch = [pltpu.VMEM((slots * rows, width), f32), pltpu.VMEM((rows, width, width), f32)]

    def exchange(send):
        send = send.reshape(devices, rows + 1, 1, width)
        return lax.all_to_all(send, PART, 0, 0, tiled=True).reshape(devices * (rows + 1), width)

    part, tile = column_part.T, column_tile.T
    sems = [pltpu.SemaphoreType.DMA((n,)) for n in (4, rows // 8, rows // 8)] + [pltpu.SemaphoreType.DMA]
    send, own, band, spread, halves, b, coupling, diagonal = call(
        functools.partial(first_kernel, sizes=sizes),
        [message, vec, band_shape, spread_shape, halves_shape, vec, (coupling.shape, f32), (diagonal.shape, f32)],
        (b, jacobi, part, tile, neighbours, coupling, diagonal),
        scratch
        + [pltpu.VMEM(jacobi.shape, f32)]
        + [pltpu.VMEM(x.shape, x.dtype) for x in (part, tile, neighbours)]
        + sems,
        pltpu.HBM,
    )
    tiles = (coupling, diagonal)
    send, own, q, scale = call(
        second_kernel, [message, vec, vec, line], (exchange(send), own, b, band, spread) + tiles, scratch
    )
    send, own, twice, half, u, keep = call(
        functools.partial(third_kernel, n_cols=n_cols), [message] + [vec] * 4 + [line],
        (exchange(send), own, b, q, scale, band, spread) + tiles, scratch,
    )
    *parts, three, search, done, kept = call(
        functools.partial(fourth_kernel, n_rows=n_rows, n_cols=n_cols, n_sub=n_sub),
        [part_shape] * n_sub + [((3 * rows, width), f32), vec, vec, line],
        (exchange(send), own, b, q, twice, half, u, keep, band, halves) + tiles,
        scratch + [pltpu.VMEM((rows, width), f32)],
    )
    summed = parts[0]
    for step in range(1, n_sub):
        summed = summed + shifted(parts[step], "sub", step)
    summed = sum_over(summed, "cols")
    mine = jnp.concatenate([summed, three])
    others = [shifted(mine, "rows", step) for step in range(1, n_rows)]
    order = sorted(range(n_rows - 1), key=lambda n: (n > 1, -n if n < 2 else n))
    twice, half, total_search, dots = call(
        functools.partial(fifth_kernel, order=order, n_rows=n_rows), [vec] * 3 + [line],
        (mine, *(others[n] for n in order), kept, search, done), [pltpu.VMEM((part_size, width), f32)],
    )
    half_hat, sum_hat = call(map_kernel, [vec, vec], (half, total_search, band))
    shares = [dots] + [shifted(dots, "sub", step) for step in range(1, n_sub)]
    return tuple(call(last_kernel, [vec, vec], (twice, half, half_hat, sum_hat, *shares)))


def solution(mesh):
    lines = P(("groups", "rows", "sub"), None)
    tiles = P(("groups", "rows", "sub"), None, None)
    slots = P(("groups", "rows", "sub"), "cols")
    in_specs = (
        tiles, P(("groups", "rows", "sub"), "cols", None, None), slots, slots, P("groups", None), lines, tiles,
    )
    return jax.shard_map(on_device, mesh=mesh, in_specs=in_specs, out_specs=(lines, lines), check_vma=False)
```

```python
import functools

import jax
import jax.numpy as jnp
from jax import lax
from jax.experimental import pallas as pl
from jax.experimental.pallas import tpu as pltpu
from jax.sharding import PartitionSpec as P

BLOCK = 5
BAND = BLOCK - 1
LANES = 128
PART = ("rows", "sub", "cols")


def apply_m(band_ref, v):
    width = v.shape[1]
    z = band_ref[BAND] * v
    for d in range(-BAND, BAND + 1):
        if d:
            z = z + band_ref[d + BAND] * pltpu.roll(v, (-d) % width, 1)
    return z


def split3(x):
    hi = x.astype(jnp.bfloat16)
    rest = x - hi.astype(jnp.float32)
    mid = rest.astype(jnp.bfloat16)
    low = (rest - mid.astype(jnp.float32)).astype(jnp.bfloat16)
    return jnp.concatenate([hi, mid, low], axis=0)


def sum_lines(parts):
    line = lax.broadcasted_iota(jnp.int32, parts[0].shape, 0)
    step = 1
    while len(parts) > 1:
        low = (line // step) % 2 == 0
        parts = [
            jnp.where(low, one, two) + pltpu.roll(jnp.where(low, two, one), step, 0)
            for one, two in zip(parts[::2], parts[1::2])
        ]
        step *= 2
    return parts[0]


def folded(column, tile):
    width = tile.shape[1]
    return jnp.sum((column * tile).reshape(width // 8, 8, width), axis=0)


def spread_products(z, spread_ref, coupling_ref, diagonal_ref, scratch, own_ref, before=None):
    partial_ref, column_ref = scratch
    rows, slots, width = coupling_ref.shape[:3]
    for first in range(0, rows, 8):
        if before is not None:
            before(first // 8)
        sums = [[] for _ in range(slots)]
        for r in range(first, first + 8):
            column = jnp.broadcast_to(z[r : r + 1], (width, width)).T
            column_ref[r] = column
            for k in range(slots):
                sums[k].append(folded(column, coupling_ref[r, k]))
        for k in range(slots):
            partial_ref[pl.ds(k * rows + first, 8), :] = sum_lines(sums[k])
    if before is not None:
        before(rows // 8)
    out = jnp.dot(spread_ref[...], split3(partial_ref[...]), preferred_element_type=jnp.float32)
    for first in range(0, rows, 8):
        own_ref[pl.ds(first, 8), :] = sum_lines([folded(column_ref[r], diagonal_ref[r]) for r in range(first, first + 8)])
    return out


def emit(z, tail, spread_ref, coupling_ref, diagonal_ref, scratch, own_ref, send_ref, before=None):
    rows = z.shape[0]
    send_ref[...] = spread_products(z, spread_ref, coupling_ref, diagonal_ref, scratch, own_ref, before)
    if callable(tail):
        tail = tail()
    for d in range(send_ref.shape[0] // (rows + 1)):
        send_ref[pl.ds(d * (rows + 1) + rows, 1), :] = tail


def pack(scalars, width):
    lane = lax.broadcasted_iota(jnp.int32, (1, width), 1)
    tail = jnp.zeros((1, width), jnp.float32)
    for at, value in enumerate(scalars):
        tail = jnp.where(lane == at, value, tail)
    return tail


def total(x):
    return jnp.sum(jnp.sum(x, axis=0, keepdims=True), axis=1, keepdims=True)


def peak(x):
    return jnp.max(jnp.max(jnp.abs(x), axis=0, keepdims=True), axis=1, keepdims=True)


def pairwise(join, items):
    items = list(items)
    while len(items) > 1:
        items = [join(*items[n : n + 2]) if n + 1 < len(items) else items[n] for n in range(0, len(items), 2)]
    return items[0]


def tails_of(recv_ref, rows):
    count = recv_ref.shape[0] // (rows + 1)
    return [recv_ref[pl.ds(d * (rows + 1) + rows, 1), :] for d in range(count)]


def chunk(recv_ref, d, rows):
    return recv_ref[pl.ds(d * (rows + 1), rows), :]


def chunks_of(recv_ref, own_in):
    rows = own_in.shape[0]
    return pairwise(jnp.add, [own_in[...]] + [chunk(recv_ref, d, rows) for d in range(recv_ref.shape[0] // (rows + 1))])


def first_kernel(
    b_hbm, jacobi_hbm, part_hbm, tile_hbm, near_hbm, coupling_hbm, diagonal_hbm,
    send_ref, own_ref, band_ref, spread_ref, halves_ref, b_ref, coupling_ref, diagonal_ref,
    partial_ref, column_ref, jacobi_ref, part_ref, tile_ref, near_ref, small_sem, jacobi_sem, coupling_sem, diagonal_sem,
    *, sizes,
):
    n_rows, n_cols, n_sub = sizes
    rows, slots = coupling_ref.shape[0], coupling_ref.shape[1]
    width = b_ref.shape[1]
    groups = rows // 8

    def some(ref, g):
        return ref.at[pl.ds(g * 8, 8)]

    def copy_of(g, source, target, sem):
        return pltpu.make_async_copy(some(source, g), some(target, g), sem.at[g])

    small = [
        pltpu.make_async_copy(source, target, small_sem.at[n])
        for n, (source, target) in enumerate(
            ((b_hbm, b_ref), (part_hbm, part_ref), (tile_hbm, tile_ref), (near_hbm, near_ref))
        )
    ]
    for copy in small:
        copy.start()
    for g in range(groups):
        copy_of(g, jacobi_hbm, jacobi_ref, jacobi_sem).start()
    for g in range(groups):
        copy_of(g, coupling_hbm, coupling_ref, coupling_sem).start()
    diagonal_copy = pltpu.make_async_copy(diagonal_hbm, diagonal_ref, diagonal_sem)
    diagonal_copy.start()
    for copy in small:
        copy.wait()
    own = lax.axis_index("rows")
    part, tile, near = part_ref[...], tile_ref[...], near_ref[...]
    near_row = lax.broadcasted_iota(jnp.int32, near.shape, 0)
    mine = jnp.sum(jnp.where(near_row == own, near, 0), axis=0, keepdims=True)
    target = jnp.where(part == 0, own, 0)
    for n in range(near.shape[1]):
        target = target + jnp.where(part == n + 1, mine[:, n : n + 1], 0)
    landing = target * (rows * n_sub) + tile
    landing = jnp.concatenate([landing[k : k + 1] for k in range(slots)] * 3, axis=1)
    at = lax.broadcasted_iota(jnp.int32, (spread_ref.shape[0], 1), 0)
    device, line = at // (rows + 1), at % (rows + 1)
    row, sub = device // (n_cols * n_sub), device // n_cols % n_sub
    wanted = jnp.where(line < rows, row * (rows * n_sub) + sub * rows + line, -1)
    spread_ref[...] = jnp.where(landing == wanted, 1.0, 0.0).astype(jnp.bfloat16)
    at = lax.broadcasted_iota(jnp.int32, (halves_ref.shape[0], 1), 0)
    size = halves_ref.shape[0] // n_sub
    sub, at = partner(lax.axis_index("sub"), at // size, n_sub), at % size
    wanted = jnp.where(at < n_rows * rows, at // rows * (rows * n_sub) + sub * rows + at % rows, -1)
    halves_ref[...] = jnp.where(landing == wanted, 1.0, 0.0).astype(jnp.bfloat16)
    m = lax.broadcasted_iota(jnp.int32, (1, 8, width), 1)
    j = lax.broadcasted_iota(jnp.int32, (1, 8, width), 2)
    last = width // BLOCK * BLOCK
    for g in range(groups):
        copy_of(g, jacobi_hbm, jacobi_ref, jacobi_sem).wait()
        folded = jnp.sum(some(jacobi_ref, g)[...].reshape(8, width // 8, 8, width), axis=1)
        for d in range(-BAND, BAND + 1):
            i = j + d
            inside = (i // BLOCK == j // BLOCK) & (j < last) if d else j >= 0
            picked = inside & (i >= 0) & (lax.rem(i + 8, 8) == m)
            band_ref[d + BAND, pl.ds(g * 8, 8)] = jnp.sum(jnp.where(picked, folded, 0.0), axis=1)
    z = apply_m(band_ref, b_ref[...])

    def before(g):
        (copy_of(g, coupling_hbm, coupling_ref, coupling_sem) if g < groups else diagonal_copy).wait()

    def tail():
        return pack([peak(b_ref[...]), jnp.maximum(peak(partial_ref[...]), peak(own_ref[...]))], width)

    emit(z, tail, spread_ref, coupling_ref, diagonal_ref, (partial_ref, column_ref), own_ref, send_ref, before)


def second_kernel(
    recv_ref, own_in, b_ref, band_ref, spread_ref, coupling_ref, diagonal_ref,
    send_ref, own_ref, q_ref, scale_ref, partial_ref, column_ref,
):
    b = b_ref[...]
    rows, width = b.shape
    top = pairwise(jnp.maximum, tails_of(recv_ref, rows))
    size, reach = top[:, 0:1], top[:, 1:2]
    good = (size > 0) & (reach > 0)
    scale, back = jnp.where(good, size / reach, 1.0), jnp.where(good, reach / size, 1.0)
    q = chunks_of(recv_ref, own_in)
    q_ref[...] = q
    scale_ref[...] = pack([scale, back], width)
    tail = pack([total(b * b), total(b * q)], width)
    z = apply_m(band_ref, scale * q)
    emit(z, tail, spread_ref, coupling_ref, diagonal_ref, (partial_ref, column_ref), own_ref, send_ref)


def scalars_of(recv_ref, rows, count, repeats):
    summed = pairwise(jnp.add, tails_of(recv_ref, rows)) * (1.0 / repeats)
    return [summed[:, n : n + 1] for n in range(count)]


def third_kernel(
    recv_ref, own_in, b_ref, q_ref, scale_ref, band_ref, spread_ref, coupling_ref, diagonal_ref,
    send_ref, own_ref, twice_ref, half_ref, u_ref, keep_ref, partial_ref, column_ref, *, n_cols,
):
    b, q = b_ref[...], q_ref[...]
    rows, width = b.shape
    rho, cross = scalars_of(recv_ref, rows, 2, n_cols)
    alpha = rho / cross
    scale, back = scale_ref[:, 0:1], scale_ref[:, 1:2]
    u = (alpha * back) * chunks_of(recv_ref, own_in)
    twice = q - u
    half = b - alpha * q
    tail = pack([total(twice * half), total(twice * twice), total(b * half), total(b * twice)], width)
    twice_ref[...], half_ref[...], u_ref[...] = twice, half, u
    keep_ref[...] = pack([rho, alpha, scale, back], width)
    z = apply_m(band_ref, scale * twice)
    emit(z, tail, spread_ref, coupling_ref, diagonal_ref, (partial_ref, column_ref), own_ref, send_ref)


def fourth_kernel(
    recv_ref, own_in, b_ref, q_ref, twice_ref, half_ref, u_ref, keep_ref, band_ref, halves_ref, coupling_ref,
    diagonal_ref, *refs, n_rows, n_cols, n_sub,
):
    parts, (three_ref, search_ref, done_ref, kept_ref, partial_ref, column_ref, own_ref) = refs[:n_sub], refs[n_sub:]
    b, q, twice, half = b_ref[...], q_ref[...], twice_ref[...], half_ref[...]
    rows, width = b.shape
    rho, alpha, scale, back = (keep_ref[:, n : n + 1] for n in range(4))
    cross, square, b_half, b_twice = scalars_of(recv_ref, rows, 4, n_cols)
    omega = cross / square
    rho_next = b_half - omega * b_twice
    ratio = rho_next / rho
    beta = ratio * (alpha / omega)
    a = twice - (omega * back) * chunks_of(recv_ref, own_in)
    residual = half - omega * twice
    image = a + beta * q - ratio * u_ref[...]
    three_ref[...] = jnp.concatenate([a, residual, image], axis=0)
    search_ref[...] = residual + beta * (b - omega * q)
    done_ref[...] = alpha * b + omega * half
    kept_ref[...] = pack([rho_next, back], width)
    first = lax.axis_index("cols") == 0
    tail = pack([jnp.where(first, total(b * image), 0.0)], width)
    z = apply_m(band_ref, scale * image)
    out = spread_products(z, halves_ref, coupling_ref, diagonal_ref, (partial_ref, column_ref), own_ref)
    size = parts[0].shape[0]
    for t, part_ref in enumerate(parts):
        part_ref[...] = out[t * size : (t + 1) * size]
        part_ref[pl.ds(n_rows * rows, 1), :] = tail
    here = pl.ds(pl.multiple_of(lax.axis_index("rows") * rows, rows), rows)
    parts[0][here, :] = parts[0][here, :] + jnp.where(first, own_ref[...], 0.0)


def fifth_kernel(mine_ref, *refs, order, n_rows):
    others, (kept_ref, search_ref, done_ref, twice_ref, half_ref, sum_ref, dots_ref, full_ref) = (
        refs[: n_rows - 1],
        refs[n_rows - 1 :],
    )
    rows, width = search_ref.shape
    size = full_ref.shape[0]
    full = mine_ref[pl.ds(0, size), :]
    for other in others:
        full = full + other[pl.ds(0, size), :]
    full_ref[...] = full
    tail = full[n_rows * rows : n_rows * rows + 1]
    alpha = kept_ref[:, 0:1] / tail[:, 0:1]
    factor = alpha * kept_ref[:, 1:2]
    own = lax.axis_index("rows")
    cross = square = None
    for step, source in [(0, mine_ref)] + [(n + 1, other) for n, other in zip(order, others)]:
        at = own if step == 0 else sender(own, step, n_rows)
        a, residual, image = (source[pl.ds(size + n * rows, rows), :] for n in range(3))
        twice = a - factor * full_ref[pl.ds(pl.multiple_of(at * rows, rows), rows), :]
        half = residual - alpha * image
        if step == 0:
            twice_ref[...], half_ref[...] = twice, half
            cross, square = twice * half, twice * twice
        else:
            cross, square = cross + twice * half, square + twice * twice
    sum_ref[...] = done_ref[...] + alpha * search_ref[...]
    dots_ref[...] = pack([total(cross), total(square)], width)


def map_kernel(half_ref, sum_ref, band_ref, half_hat_ref, sum_hat_ref):
    half_hat_ref[...] = apply_m(band_ref, half_ref[...])
    sum_hat_ref[...] = apply_m(band_ref, sum_ref[...])


def last_kernel(twice_ref, half_ref, half_hat_ref, sum_hat_ref, *refs):
    *shares, solution_ref, residual_ref = refs
    dots = functools.reduce(jnp.add, [share[...] for share in shares])
    omega = dots[:, 0:1] / dots[:, 1:2]
    residual_ref[...] = half_ref[...] - omega * twice_ref[...]
    solution_ref[...] = sum_hat_ref[...] + omega * half_hat_ref[...]


def partner(at, step, count):
    return at ^ step if count & (count - 1) == 0 else (at + step) % count


def sender(at, step, count):
    return at ^ step if count & (count - 1) == 0 else (at + count - step) % count


def shifted(x, axis, step):
    count = lax.axis_size(axis)
    return lax.ppermute(x, axis, [(i, partner(i, step, count)) for i in range(count)])


def sum_over(x, axis):
    out = x
    for step in range(1, lax.axis_size(axis)):
        out = out + shifted(x, axis, step)
    return out


def call(kernel, outs, args, scratch=(), space=pltpu.VMEM):
    spec = pl.BlockSpec(memory_space=pltpu.VMEM)
    if space == pltpu.HBM:
        args = [pltpu.with_memory_space_constraint(x, space) for x in args]
    return pl.pallas_call(
        kernel,
        out_shape=[pltpu.VMEM(shape, kind) if space == pltpu.HBM else jax.ShapeDtypeStruct(shape, kind) for shape, kind in outs],
        in_specs=[pl.BlockSpec(memory_space=space)] * len(args),
        out_specs=[spec] * len(outs),
        scratch_shapes=list(scratch),
        compiler_params=pltpu.CompilerParams(vmem_limit_bytes=24 << 20),
    )(*args)


def on_device(diagonal, coupling, column_part, column_tile, neighbours, b, jacobi):
    f32 = jnp.float32
    rows, width = b.shape
    slots = coupling.shape[1]
    sizes = tuple(lax.axis_size(axis) for axis in ("rows", "cols", "sub"))
    n_rows, n_cols, n_sub = sizes
    devices = n_rows * n_cols * n_sub
    vec, line = ((rows, width), f32), ((1, width), f32)
    message = ((devices * (rows + 1), width), f32)
    part_size = n_rows * rows + 8
    part_shape = ((part_size, width), f32)
    band_shape = ((2 * BAND + 1, rows, width), f32)
    spread_shape = ((devices * (rows + 1), 3 * slots * rows), jnp.bfloat16)
    halves_shape = ((n_sub * part_size, 3 * slots * rows), jnp.bfloat16)
    scratch = [pltpu.VMEM((slots * rows, width), f32), pltpu.VMEM((rows, width, width), f32)]

    def exchange(send):
        send = send.reshape(devices, rows + 1, 1, width)
        return lax.all_to_all(send, PART, 0, 0, tiled=True).reshape(devices * (rows + 1), width)

    part, tile = column_part.T, column_tile.T
    sems = [pltpu.SemaphoreType.DMA((n,)) for n in (4, rows // 8, rows // 8)] + [pltpu.SemaphoreType.DMA]
    send, own, band, spread, halves, b, coupling, diagonal = call(
        functools.partial(first_kernel, sizes=sizes),
        [message, vec, band_shape, spread_shape, halves_shape, vec, (coupling.shape, f32), (diagonal.shape, f32)],
        (b, jacobi, part, tile, neighbours, coupling, diagonal),
        scratch
        + [pltpu.VMEM(jacobi.shape, f32)]
        + [pltpu.VMEM(x.shape, x.dtype) for x in (part, tile, neighbours)]
        + sems,
        pltpu.HBM,
    )
    tiles = (coupling, diagonal)
    send, own, q, scale = call(
        second_kernel, [message, vec, vec, line], (exchange(send), own, b, band, spread) + tiles, scratch
    )
    send, own, twice, half, u, keep = call(
        functools.partial(third_kernel, n_cols=n_cols), [message] + [vec] * 4 + [line],
        (exchange(send), own, b, q, scale, band, spread) + tiles, scratch,
    )
    *parts, three, search, done, kept = call(
        functools.partial(fourth_kernel, n_rows=n_rows, n_cols=n_cols, n_sub=n_sub),
        [part_shape] * n_sub + [((3 * rows, width), f32), vec, vec, line],
        (exchange(send), own, b, q, twice, half, u, keep, band, halves) + tiles,
        scratch + [pltpu.VMEM((rows, width), f32)],
    )
    summed = parts[0]
    for step in range(1, n_sub):
        summed = summed + shifted(parts[step], "sub", step)
    summed = sum_over(summed, "cols")
    mine = jnp.concatenate([summed, three])
    others = [shifted(mine, "rows", step) for step in range(1, n_rows)]
    order = sorted(range(n_rows - 1), key=lambda n: (n > 1, -n if n < 2 else n))
    twice, half, total_search, dots = call(
        functools.partial(fifth_kernel, order=order, n_rows=n_rows), [vec] * 3 + [line],
        (mine, *(others[n] for n in order), kept, search, done), [pltpu.VMEM((part_size, width), f32)],
    )
    half_hat, sum_hat = call(map_kernel, [vec, vec], (half, total_search, band))
    shares = [dots] + [shifted(dots, "sub", step) for step in range(1, n_sub)]
    return tuple(call(last_kernel, [vec, vec], (twice, half, half_hat, sum_hat, *shares)))


def solution(mesh):
    lines = P(("groups", "rows", "sub"), None)
    tiles = P(("groups", "rows", "sub"), None, None)
    slots = P(("groups", "rows", "sub"), "cols")
    in_specs = (
        tiles, P(("groups", "rows", "sub"), "cols", None, None), slots, slots, P("groups", None), lines, tiles,
    )
    return jax.shard_map(on_device, mesh=mesh, in_specs=in_specs, out_specs=(lines, lines), check_vma=False)
```

```python
import functools

import jax
import jax.numpy as jnp
from jax import lax
from jax.experimental import pallas as pl
from jax.experimental.pallas import tpu as pltpu
from jax.sharding import PartitionSpec as P

BLOCK = 5
BAND = BLOCK - 1
LANES = 128
PART = ("rows", "sub", "cols")


def apply_m(band_ref, v):
    width = v.shape[1]
    z = band_ref[BAND] * v
    for d in range(-BAND, BAND + 1):
        if d:
            z = z + band_ref[d + BAND] * pltpu.roll(v, (-d) % width, 1)
    return z


def split3(x):
    hi = x.astype(jnp.bfloat16)
    rest = x - hi.astype(jnp.float32)
    mid = rest.astype(jnp.bfloat16)
    low = (rest - mid.astype(jnp.float32)).astype(jnp.bfloat16)
    return jnp.concatenate([hi, mid, low], axis=0)


def sum_lines(parts):
    line = lax.broadcasted_iota(jnp.int32, parts[0].shape, 0)
    step = 1
    while len(parts) > 1:
        low = (line // step) % 2 == 0
        parts = [
            jnp.where(low, one, two) + pltpu.roll(jnp.where(low, two, one), step, 0)
            for one, two in zip(parts[::2], parts[1::2])
        ]
        step *= 2
    return parts[0]


def folded(column, tile):
    width = tile.shape[1]
    return jnp.sum((column * tile).reshape(width // 8, 8, width), axis=0)


def spread_products(z, spread_ref, coupling_ref, diagonal_ref, scratch, own_ref, before=None):
    partial_ref, column_ref = scratch
    rows, slots, width = coupling_ref.shape[:3]
    for first in range(0, rows, 8):
        if before is not None:
            before(first // 8)
        sums = [[] for _ in range(slots)]
        for r in range(first, first + 8):
            column = jnp.broadcast_to(z[r : r + 1], (width, width)).T
            column_ref[r] = column
            for k in range(slots):
                sums[k].append(folded(column, coupling_ref[r, k]))
        for k in range(slots):
            partial_ref[pl.ds(k * rows + first, 8), :] = sum_lines(sums[k])
    if before is not None:
        before(rows // 8)
    out = jnp.dot(spread_ref[...], split3(partial_ref[...]), preferred_element_type=jnp.float32)
    for first in range(0, rows, 8):
        own_ref[pl.ds(first, 8), :] = sum_lines([folded(column_ref[r], diagonal_ref[r]) for r in range(first, first + 8)])
    return out


def emit(z, tail, spread_ref, coupling_ref, diagonal_ref, scratch, own_ref, send_ref, before=None):
    rows = z.shape[0]
    send_ref[...] = spread_products(z, spread_ref, coupling_ref, diagonal_ref, scratch, own_ref, before)
    if callable(tail):
        tail = tail()
    for d in range(send_ref.shape[0] // (rows + 1)):
        send_ref[pl.ds(d * (rows + 1) + rows, 1), :] = tail


def pack(scalars, width):
    lane = lax.broadcasted_iota(jnp.int32, (1, width), 1)
    tail = jnp.zeros((1, width), jnp.float32)
    for at, value in enumerate(scalars):
        tail = jnp.where(lane == at, value, tail)
    return tail


def total(x):
    return jnp.sum(jnp.sum(x, axis=0, keepdims=True), axis=1, keepdims=True)


def peak(x):
    return jnp.max(jnp.max(jnp.abs(x), axis=0, keepdims=True), axis=1, keepdims=True)


def pairwise(join, items):
    items = list(items)
    while len(items) > 1:
        items = [join(*items[n : n + 2]) if n + 1 < len(items) else items[n] for n in range(0, len(items), 2)]
    return items[0]


def tails_of(recv_ref, rows):
    count = recv_ref.shape[0] // (rows + 1)
    return [recv_ref[pl.ds(d * (rows + 1) + rows, 1), :] for d in range(count)]


def chunk(recv_ref, d, rows):
    return recv_ref[pl.ds(d * (rows + 1), rows), :]


def chunks_of(recv_ref, own_in):
    rows = own_in.shape[0]
    return pairwise(jnp.add, [own_in[...]] + [chunk(recv_ref, d, rows) for d in range(recv_ref.shape[0] // (rows + 1))])


def first_kernel(
    b_hbm, jacobi_hbm, part_hbm, tile_hbm, near_hbm, coupling_hbm, diagonal_hbm,
    send_ref, own_ref, band_ref, spread_ref, halves_ref, b_ref, coupling_ref, diagonal_ref,
    partial_ref, column_ref, jacobi_ref, part_ref, tile_ref, near_ref, small_sem, jacobi_sem, coupling_sem, diagonal_sem,
    *, sizes,
):
    n_rows, n_cols, n_sub = sizes
    rows, slots = coupling_ref.shape[0], coupling_ref.shape[1]
    width = b_ref.shape[1]
    groups = rows // 8

    def some(ref, g):
        return ref.at[pl.ds(g * 8, 8)]

    def copy_of(g, source, target, sem):
        return pltpu.make_async_copy(some(source, g), some(target, g), sem.at[g])

    small = [
        pltpu.make_async_copy(source, target, small_sem.at[n])
        for n, (source, target) in enumerate(
            ((b_hbm, b_ref), (part_hbm, part_ref), (tile_hbm, tile_ref), (near_hbm, near_ref))
        )
    ]
    for copy in small:
        copy.start()
    for g in range(groups):
        copy_of(g, jacobi_hbm, jacobi_ref, jacobi_sem).start()
    for g in range(groups):
        copy_of(g, coupling_hbm, coupling_ref, coupling_sem).start()
    diagonal_copy = pltpu.make_async_copy(diagonal_hbm, diagonal_ref, diagonal_sem)
    diagonal_copy.start()
    for copy in small:
        copy.wait()
    own = lax.axis_index("rows")
    part, tile, near = part_ref[...], tile_ref[...], near_ref[...]
    near_row = lax.broadcasted_iota(jnp.int32, near.shape, 0)
    mine = jnp.sum(jnp.where(near_row == own, near, 0), axis=0, keepdims=True)
    target = jnp.where(part == 0, own, 0)
    for n in range(near.shape[1]):
        target = target + jnp.where(part == n + 1, mine[:, n : n + 1], 0)
    landing = target * (rows * n_sub) + tile
    landing = jnp.concatenate([landing[k : k + 1] for k in range(slots)] * 3, axis=1)
    at = lax.broadcasted_iota(jnp.int32, (spread_ref.shape[0], 1), 0)
    device, line = at // (rows + 1), at % (rows + 1)
    row, sub = device // (n_cols * n_sub), device // n_cols % n_sub
    wanted = jnp.where(line < rows, row * (rows * n_sub) + sub * rows + line, -1)
    spread_ref[...] = jnp.where(landing == wanted, 1.0, 0.0).astype(jnp.bfloat16)
    at = lax.broadcasted_iota(jnp.int32, (halves_ref.shape[0], 1), 0)
    size = halves_ref.shape[0] // n_sub
    sub, at = partner(lax.axis_index("sub"), at // size, n_sub), at % size
    wanted = jnp.where(at < n_rows * rows, at // rows * (rows * n_sub) + sub * rows + at % rows, -1)
    halves_ref[...] = jnp.where(landing == wanted, 1.0, 0.0).astype(jnp.bfloat16)
    m = lax.broadcasted_iota(jnp.int32, (1, 8, width), 1)
    j = lax.broadcasted_iota(jnp.int32, (1, 8, width), 2)
    last = width // BLOCK * BLOCK
    for g in range(groups):
        copy_of(g, jacobi_hbm, jacobi_ref, jacobi_sem).wait()
        folded = jnp.sum(some(jacobi_ref, g)[...].reshape(8, width // 8, 8, width), axis=1)
        for d in range(-BAND, BAND + 1):
            i = j + d
            inside = (i // BLOCK == j // BLOCK) & (j < last) if d else j >= 0
            picked = inside & (i >= 0) & (lax.rem(i + 8, 8) == m)
            band_ref[d + BAND, pl.ds(g * 8, 8)] = jnp.sum(jnp.where(picked, folded, 0.0), axis=1)
    z = apply_m(band_ref, b_ref[...])

    def before(g):
        (copy_of(g, coupling_hbm, coupling_ref, coupling_sem) if g < groups else diagonal_copy).wait()

    def tail():
        return pack([peak(b_ref[...]), jnp.maximum(peak(partial_ref[...]), peak(own_ref[...]))], width)

    emit(z, tail, spread_ref, coupling_ref, diagonal_ref, (partial_ref, column_ref), own_ref, send_ref, before)


def second_kernel(
    recv_ref, own_in, b_ref, band_ref, spread_ref, coupling_ref, diagonal_ref,
    send_ref, own_ref, q_ref, scale_ref, partial_ref, column_ref,
):
    b = b_ref[...]
    rows, width = b.shape
    top = pairwise(jnp.maximum, tails_of(recv_ref, rows))
    size, reach = top[:, 0:1], top[:, 1:2]
    good = (size > 0) & (reach > 0)
    scale, back = jnp.where(good, size / reach, 1.0), jnp.where(good, reach / size, 1.0)
    q = chunks_of(recv_ref, own_in)
    q_ref[...] = q
    scale_ref[...] = pack([scale, back], width)
    tail = pack([total(b * b), total(b * q)], width)
    z = apply_m(band_ref, scale * q)
    emit(z, tail, spread_ref, coupling_ref, diagonal_ref, (partial_ref, column_ref), own_ref, send_ref)


def scalars_of(recv_ref, rows, count, repeats):
    summed = pairwise(jnp.add, tails_of(recv_ref, rows)) * (1.0 / repeats)
    return [summed[:, n : n + 1] for n in range(count)]


def third_kernel(
    recv_ref, own_in, b_ref, q_ref, scale_ref, band_ref, spread_ref, coupling_ref, diagonal_ref,
    send_ref, own_ref, twice_ref, half_ref, u_ref, keep_ref, partial_ref, column_ref, *, n_cols,
):
    b, q = b_ref[...], q_ref[...]
    rows, width = b.shape
    rho, cross = scalars_of(recv_ref, rows, 2, n_cols)
    alpha = rho / cross
    scale, back = scale_ref[:, 0:1], scale_ref[:, 1:2]
    u = (alpha * back) * chunks_of(recv_ref, own_in)
    twice = q - u
    half = b - alpha * q
    tail = pack([total(twice * half), total(twice * twice), total(b * half), total(b * twice)], width)
    twice_ref[...], half_ref[...], u_ref[...] = twice, half, u
    keep_ref[...] = pack([rho, alpha, scale, back], width)
    z = apply_m(band_ref, scale * twice)
    emit(z, tail, spread_ref, coupling_ref, diagonal_ref, (partial_ref, column_ref), own_ref, send_ref)


def fourth_kernel(
    recv_ref, own_in, b_ref, q_ref, twice_ref, half_ref, u_ref, keep_ref, band_ref, halves_ref, coupling_ref,
    diagonal_ref, *refs, n_rows, n_cols, n_sub,
):
    parts, (three_ref, search_ref, done_ref, kept_ref, partial_ref, column_ref, own_ref) = refs[:n_sub], refs[n_sub:]
    b, q, twice, half = b_ref[...], q_ref[...], twice_ref[...], half_ref[...]
    rows, width = b.shape
    rho, alpha, scale, back = (keep_ref[:, n : n + 1] for n in range(4))
    cross, square, b_half, b_twice = scalars_of(recv_ref, rows, 4, n_cols)
    omega = cross / square
    rho_next = b_half - omega * b_twice
    ratio = rho_next / rho
    beta = ratio * (alpha * (square / cross))
    a = twice - (omega * back) * chunks_of(recv_ref, own_in)
    residual = half - omega * twice
    image = a + beta * q - ratio * u_ref[...]
    three_ref[...] = jnp.concatenate([a, residual, image], axis=0)
    search_ref[...] = residual + beta * (b - omega * q)
    done_ref[...] = alpha * b + omega * half
    kept_ref[...] = pack([rho_next, back], width)
    first = lax.axis_index("cols") == 0
    tail = pack([jnp.where(first, total(b * image), 0.0)], width)
    z = apply_m(band_ref, scale * image)
    out = spread_products(z, halves_ref, coupling_ref, diagonal_ref, (partial_ref, column_ref), own_ref)
    size = parts[0].shape[0]
    for t, part_ref in enumerate(parts):
        part_ref[...] = out[t * size : (t + 1) * size]
        part_ref[pl.ds(n_rows * rows, 1), :] = tail
    here = pl.ds(pl.multiple_of(lax.axis_index("rows") * rows, rows), rows)
    parts[0][here, :] = parts[0][here, :] + jnp.where(first, own_ref[...], 0.0)


def fifth_kernel(mine_ref, *refs, order, n_rows):
    others, (kept_ref, search_ref, done_ref, twice_ref, half_ref, sum_ref, dots_ref, full_ref) = (
        refs[: n_rows - 1],
        refs[n_rows - 1 :],
    )
    rows, width = search_ref.shape
    size = full_ref.shape[0]
    full = mine_ref[pl.ds(0, size), :]
    for other in others:
        full = full + other[pl.ds(0, size), :]
    full_ref[...] = full
    tail = full[n_rows * rows : n_rows * rows + 1]
    alpha = kept_ref[:, 0:1] / tail[:, 0:1]
    factor = alpha * kept_ref[:, 1:2]
    own = lax.axis_index("rows")
    cross = square = None
    for step, source in [(0, mine_ref)] + [(n + 1, other) for n, other in zip(order, others)]:
        at = own if step == 0 else sender(own, step, n_rows)
        a, residual, image = (source[pl.ds(size + n * rows, rows), :] for n in range(3))
        twice = a - factor * full_ref[pl.ds(pl.multiple_of(at * rows, rows), rows), :]
        half = residual - alpha * image
        if step == 0:
            twice_ref[...], half_ref[...] = twice, half
            cross, square = twice * half, twice * twice
        else:
            cross, square = cross + twice * half, square + twice * twice
    sum_ref[...] = done_ref[...] + alpha * search_ref[...]
    dots_ref[...] = pack([total(cross), total(square)], width)


def map_kernel(half_ref, sum_ref, band_ref, half_hat_ref, sum_hat_ref):
    half_hat_ref[...] = apply_m(band_ref, half_ref[...])
    sum_hat_ref[...] = apply_m(band_ref, sum_ref[...])


def last_kernel(twice_ref, half_ref, half_hat_ref, sum_hat_ref, *refs):
    *shares, solution_ref, residual_ref = refs
    dots = functools.reduce(jnp.add, [share[...] for share in shares])
    omega = dots[:, 0:1] / dots[:, 1:2]
    residual_ref[...] = half_ref[...] - omega * twice_ref[...]
    solution_ref[...] = sum_hat_ref[...] + omega * half_hat_ref[...]


def partner(at, step, count):
    return at ^ step if count & (count - 1) == 0 else (at + step) % count


def sender(at, step, count):
    return at ^ step if count & (count - 1) == 0 else (at + count - step) % count


def shifted(x, axis, step):
    count = lax.axis_size(axis)
    return lax.ppermute(x, axis, [(i, partner(i, step, count)) for i in range(count)])


def sum_over(x, axis):
    out = x
    for step in range(1, lax.axis_size(axis)):
        out = out + shifted(x, axis, step)
    return out


def call(kernel, outs, args, scratch=(), space=pltpu.VMEM):
    spec = pl.BlockSpec(memory_space=pltpu.VMEM)
    if space == pltpu.HBM:
        args = [pltpu.with_memory_space_constraint(x, space) for x in args]
    return pl.pallas_call(
        kernel,
        out_shape=[pltpu.VMEM(shape, kind) if space == pltpu.HBM else jax.ShapeDtypeStruct(shape, kind) for shape, kind in outs],
        in_specs=[pl.BlockSpec(memory_space=space)] * len(args),
        out_specs=[spec] * len(outs),
        scratch_shapes=list(scratch),
        compiler_params=pltpu.CompilerParams(vmem_limit_bytes=24 << 20),
    )(*args)


def on_device(diagonal, coupling, column_part, column_tile, neighbours, b, jacobi):
    f32 = jnp.float32
    rows, width = b.shape
    slots = coupling.shape[1]
    sizes = tuple(lax.axis_size(axis) for axis in ("rows", "cols", "sub"))
    n_rows, n_cols, n_sub = sizes
    devices = n_rows * n_cols * n_sub
    vec, line = ((rows, width), f32), ((1, width), f32)
    message = ((devices * (rows + 1), width), f32)
    part_size = n_rows * rows + 8
    part_shape = ((part_size, width), f32)
    band_shape = ((2 * BAND + 1, rows, width), f32)
    spread_shape = ((devices * (rows + 1), 3 * slots * rows), jnp.bfloat16)
    halves_shape = ((n_sub * part_size, 3 * slots * rows), jnp.bfloat16)
    scratch = [pltpu.VMEM((slots * rows, width), f32), pltpu.VMEM((rows, width, width), f32)]

    def exchange(send):
        send = send.reshape(devices, rows + 1, 1, width)
        return lax.all_to_all(send, PART, 0, 0, tiled=True).reshape(devices * (rows + 1), width)

    part, tile = column_part.T, column_tile.T
    sems = [pltpu.SemaphoreType.DMA((n,)) for n in (4, rows // 8, rows // 8)] + [pltpu.SemaphoreType.DMA]
    send, own, band, spread, halves, b, coupling, diagonal = call(
        functools.partial(first_kernel, sizes=sizes),
        [message, vec, band_shape, spread_shape, halves_shape, vec, (coupling.shape, f32), (diagonal.shape, f32)],
        (b, jacobi, part, tile, neighbours, coupling, diagonal),
        scratch
        + [pltpu.VMEM(jacobi.shape, f32)]
        + [pltpu.VMEM(x.shape, x.dtype) for x in (part, tile, neighbours)]
        + sems,
        pltpu.HBM,
    )
    tiles = (coupling, diagonal)
    send, own, q, scale = call(
        second_kernel, [message, vec, vec, line], (exchange(send), own, b, band, spread) + tiles, scratch
    )
    send, own, twice, half, u, keep = call(
        functools.partial(third_kernel, n_cols=n_cols), [message] + [vec] * 4 + [line],
        (exchange(send), own, b, q, scale, band, spread) + tiles, scratch,
    )
    *parts, three, search, done, kept = call(
        functools.partial(fourth_kernel, n_rows=n_rows, n_cols=n_cols, n_sub=n_sub),
        [part_shape] * n_sub + [((3 * rows, width), f32), vec, vec, line],
        (exchange(send), own, b, q, twice, half, u, keep, band, halves) + tiles,
        scratch + [pltpu.VMEM((rows, width), f32)],
    )
    summed = parts[0]
    for step in range(1, n_sub):
        summed = summed + shifted(parts[step], "sub", step)
    summed = sum_over(summed, "cols")
    mine = jnp.concatenate([summed, three])
    others = [shifted(mine, "rows", step) for step in range(1, n_rows)]
    order = sorted(range(n_rows - 1), key=lambda n: (n > 1, -n if n < 2 else n))
    twice, half, total_search, dots = call(
        functools.partial(fifth_kernel, order=order, n_rows=n_rows), [vec] * 3 + [line],
        (mine, *(others[n] for n in order), kept, search, done), [pltpu.VMEM((part_size, width), f32)],
    )
    half_hat, sum_hat = call(map_kernel, [vec, vec], (half, total_search, band))
    shares = [dots] + [shifted(dots, "sub", step) for step in range(1, n_sub)]
    return tuple(call(last_kernel, [vec, vec], (twice, half, half_hat, sum_hat, *shares)))


def solution(mesh):
    lines = P(("groups", "rows", "sub"), None)
    tiles = P(("groups", "rows", "sub"), None, None)
    slots = P(("groups", "rows", "sub"), "cols")
    in_specs = (
        tiles, P(("groups", "rows", "sub"), "cols", None, None), slots, slots, P("groups", None), lines, tiles,
    )
    return jax.shard_map(on_device, mesh=mesh, in_specs=in_specs, out_specs=(lines, lines), check_vma=False)
```
